32 devices in a mesh: seq: 16 (over z, y, x), head: 2 (over core).
Axes of the slice: x: 2, y: 2, z: 4, core: 2. Of those that a mesh axis runs over, the one named last changes fastest.
Arguments:
- queries: bfloat16 [6144, 3072], P('seq', 'head'), may hold values from -6 to 6
- keys: bfloat16 [6144, 3072], P('seq', 'head'), may hold values from -6 to 6
- values: bfloat16 [6144, 3072], P('seq', 'head'), may hold values from -6 to 6
- text_keys: bfloat16 [512, 3072], P('seq', 'head'), may hold values from -6 to 6
- text_values: bfloat16 [512, 3072], P('seq', 'head'), may hold values from -6 to 6
- neighbours: int32 [16, 5], P('seq'), may hold values from -1 to 15, as said below
- clip_lengths: int32 [4], replicated, may hold values from 1 to 7, as said below
- text_lengths: int32 [4], replicated, may hold values from 1 to 224, as said below
- out_weight: bfloat16 [3072, 3072], P('head'), may hold values from -0.109375 to 0.109375
Outputs:
- mixed: bfloat16 [6144, 3072], P(('seq', 'head'))
The draws below stay inside these ranges and needn't reach their ends.
Inputs may be any that keep to these rules, and one draw needn't show every extreme that they name: Clips lie end to end and fill all 16 tiles; each clip is laid out in frames of 1 to 3 tiles, and a tile lists itself, its neighbours within its frame and the tiles at the same place in the frames before and after, all inside its clip. `clip_lengths`: the lengths sum to 16. `text_lengths`: A clip's text length is at most its tiles times 32; every clip of 7 tiles fills all its text slots, and every clip of one tile has one text token.
All inputs are finite; a program needn't handle non-finite values.
Results may differ from the reference program's by a relative error of at most 0.012.
Values may be sent and summed in bfloat16 or wider, within the bound.
A program may use at most 192 MiB of HBM per device.

```python
import jax
import jax.numpy as jnp
from jax import lax

D = 3072
HEADS = 24
HD = 128
TILE = 384
TXT_DEV = 32
REACH = 3
MOST = 7
CLIPS = 4
TOKENS = 6144
TEXT = 512
N_SEQ = 16
N_HEAD = 2


def clip_plan(key):
    base = jax.random.fold_in(key, 11)
    first, second, third, fourth = jax.random.split(base, 4)
    spread = jax.random.randint(first, (CLIPS // 2,), 0, 4).at[0].set(3)
    lengths = jnp.stack([4 + spread, 4 - spread], axis=1).reshape(CLIPS)
    order = jax.random.permutation(fourth, CLIPS)
    lengths = lengths[order].astype(jnp.int32)
    frames = jax.random.randint(second, (CLIPS,), 1, REACH + 1).astype(jnp.int32)
    text = jax.random.randint(third, (CLIPS,), 1, lengths * TXT_DEV + 1).astype(jnp.int32)
    text = jnp.where(lengths == MOST, lengths * TXT_DEV, text)
    text = jnp.where(lengths == 1, 1, text).astype(jnp.int32)
    starts = jnp.cumsum(lengths) - lengths
    tiles = jnp.arange(N_SEQ, dtype=jnp.int32)
    clip_of = jnp.sum((tiles[:, None] >= starts[None, :]).astype(jnp.int32), axis=1) - 1
    inner = tiles - starts[clip_of]
    width = frames[clip_of]
    count = lengths[clip_of]
    empty = jnp.full_like(tiles, -1)
    left = jnp.where(inner % width != 0, tiles - 1, empty)
    right = jnp.where(((inner + 1) % width != 0) & (inner + 1 < count), tiles + 1, empty)
    before = jnp.where(inner >= width, tiles - width, empty)
    after = jnp.where(inner + width < count, tiles + width, empty)
    listed = jnp.stack([tiles, left, right, before, after], axis=1).astype(jnp.int32)
    return (lengths, text, listed)


def draw_neighbours(key, part):
    return clip_plan(key)[2]


def draw_clip_lengths(key, part):
    return clip_plan(key)[0]


def draw_text_lengths(key, part):
    return clip_plan(key)[1]


def draw_queries(key, part):
    noise = jnp.clip(jax.random.normal(jax.random.fold_in(key, 31), (TOKENS, HEADS * HD), jnp.float32), -6.0, 6.0)
    return noise.astype(jnp.bfloat16)


def draw_keys(key, part):
    noise = jnp.clip(jax.random.normal(jax.random.fold_in(key, 37), (TOKENS, HEADS * HD), jnp.float32), -6.0, 6.0)
    return noise.astype(jnp.bfloat16)


def levels(rng, shape, cuts, low, largest):
    def one(dim, blocks):
        steps = jax.random.uniform(jax.random.fold_in(jax.random.fold_in(rng, 6), dim), (blocks,), jnp.float32, low / len(cuts), largest / len(cuts))
        return jnp.repeat(jnp.exp(steps), shape[dim] // blocks).reshape((-1,) + (1,) * (len(shape) - dim - 1))

    level = one(*cuts[0])
    for cut in cuts[1:]:
        level = level * one(*cut)
    return level


def normal_values(own_key, shape, deviation, most, cuts=(), held_as=jnp.bfloat16):
    array = jax.random.normal(own_key, shape, jnp.float32) * deviation
    if len(cuts) > 0:
        array = levels(own_key, shape, cuts, -0.22, 0.18) * array
    return jnp.clip(array, min=-most, max=most).astype(held_as)


def setup_inputs(seed: int = 0) -> dict:
    key_list = jax.random.split(jax.random.key(seed), 10)
    queries = draw_queries(jax.random.fold_in(key_list[9], 71), 0)
    keys = draw_keys(jax.random.fold_in(key_list[9], 71), 0)
    values = normal_values(key_list[2], (TOKENS, HEADS * HD), 1.0, 6.0, ((0, 16), (1, 2)))
    text_keys = normal_values(key_list[3], (TEXT, HEADS * HD), 1.0, 6.0, ((0, 16), (1, 2)))
    text_values = normal_values(key_list[4], (TEXT, HEADS * HD), 1.0, 6.0, ((0, 16), (1, 2)))
    neighbours = draw_neighbours(jax.random.fold_in(key_list[9], 71), 0)
    clip_lengths = draw_clip_lengths(jax.random.fold_in(key_list[9], 71), 0)
    text_lengths = draw_text_lengths(jax.random.fold_in(key_list[9], 71), 0)
    out_weight = normal_values(key_list[8], (HEADS * HD, D), (HEADS * HD) ** -0.5, 0.109375, ((0, 2),))
    return {"queries": queries, "keys": keys, "values": values, "text_keys": text_keys, "text_values": text_values, "neighbours": neighbours, "clip_lengths": clip_lengths, "text_lengths": text_lengths, "out_weight": out_weight}


def reference(queries, keys, values, text_keys, text_values, neighbours, clip_lengths, text_lengths, out_weight):
    starts = jnp.cumsum(clip_lengths) - clip_lengths
    tiles = jnp.arange(N_SEQ, dtype=jnp.int32)
    clip_of = (jnp.sum((tiles[:, None] >= starts[None, :]).astype(jnp.int32), axis=1) - 1).astype(jnp.int32)
    text_low = starts[clip_of] * TXT_DEV
    text_high = text_low + text_lengths[clip_of]
    span = 2 * REACH + 1
    text_span = 2 * MOST - 1
    key_pad = jnp.pad(keys, ((REACH * TILE, REACH * TILE), (0, 0)))
    value_pad = jnp.pad(values, ((REACH * TILE, REACH * TILE), (0, 0)))
    tkey_pad = jnp.pad(text_keys, (((MOST - 1) * TXT_DEV, (MOST - 1) * TXT_DEV), (0, 0)))
    tvalue_pad = jnp.pad(text_values, (((MOST - 1) * TXT_DEV, (MOST - 1) * TXT_DEV), (0, 0)))
    scale = HD ** -0.5

    def one_tile(tile):
        tile = tile.astype(jnp.int32)
        q_rows = lax.dynamic_slice_in_dim(queries, tile * TILE, TILE, 0)
        k_rows = lax.dynamic_slice_in_dim(key_pad, tile * TILE, span * TILE, 0)
        v_rows = lax.dynamic_slice_in_dim(value_pad, tile * TILE, span * TILE, 0)
        offsets = jnp.arange(span, dtype=jnp.int32) - REACH
        listed = neighbours[tile]
        present = jnp.any((listed[None, :] == (tile + offsets)[:, None]) & (listed[None, :] >= 0), axis=1)
        tile_mask = jnp.repeat(present, TILE)
        tk_rows = lax.dynamic_slice_in_dim(tkey_pad, tile * TXT_DEV, text_span * TXT_DEV, 0)
        tv_rows = lax.dynamic_slice_in_dim(tvalue_pad, tile * TXT_DEV, text_span * TXT_DEV, 0)
        global_rows = tile * TXT_DEV - (MOST - 1) * TXT_DEV + jnp.arange(text_span * TXT_DEV, dtype=jnp.int32)
        text_mask = (global_rows >= text_low[tile]) & (global_rows < text_high[tile])
        all_keys = jnp.concatenate([k_rows, tk_rows], axis=0)
        all_values = jnp.concatenate([v_rows, tv_rows], axis=0)
        mask = jnp.concatenate([tile_mask, text_mask], axis=0)
        qf = q_rows.reshape(TILE, HEADS, HD).astype(jnp.float32)
        kf = all_keys.reshape(-1, HEADS, HD).astype(jnp.float32)
        vf = all_values.reshape(-1, HEADS, HD).astype(jnp.float32)
        score = jnp.einsum("qhd,khd->hqk", qf, kf) * scale
        score = jnp.where(mask[None, None, :], score, -1e30)
        top = jnp.max(score, axis=-1)
        weight = jnp.where(mask[None, None, :], jnp.exp(score - top[..., None]), 0.0)
        total = jnp.sum(weight, axis=-1)
        rounded = lax.optimization_barrier(weight.astype(jnp.bfloat16))
        acc = jnp.einsum("hqk,khd->hqd", rounded.astype(jnp.float32), vf)
        attended = acc / total[..., None]
        return jnp.transpose(attended, (1, 0, 2)).reshape(TILE, HEADS * HD).astype(jnp.bfloat16)

    attended = lax.map(one_tile, tiles).reshape(N_SEQ * TILE, HEADS * HD)
    group = HEADS * HD // N_HEAD
    parts = attended.reshape(N_SEQ * TILE, N_HEAD, group)
    weights = out_weight.reshape(N_HEAD, group, D)

    def add_group(total, index):
        piece = jnp.dot(parts[:, index, :], weights[index], preferred_element_type=jnp.float32)
        rounded = lax.optimization_barrier(piece.astype(jnp.bfloat16))
        return total + rounded.astype(jnp.float32), None

    summed, unused = lax.scan(add_group, jnp.zeros((N_SEQ * TILE, D), jnp.float32), jnp.arange(N_HEAD, dtype=jnp.int32))
    return summed.astype(jnp.bfloat16)
```

```python
import functools

import jax
import jax.numpy as jnp
from jax import lax
from jax.experimental import pallas as pl
from jax.experimental.pallas import tpu as pltpu
from jax.sharding import PartitionSpec as P

HD = 128
REACH = 3
MOST = 7
PLANE = 4
LOW = 1e30
MESH = pl.DeviceIdType.MESH


def group_of(n_seq, heads):
    return PLANE if n_seq % PLANE == 0 and heads % PLANE == 0 else 1


def kernel(
    n_seq,
    n_head,
    near_ref,
    clip_ref,
    text_ref,
    q_hbm,
    k_hbm,
    v_hbm,
    tk_hbm,
    tv_hbm,
    w_hbm,
    out_ref,
    q,
    k,
    v,
    tk,
    tv,
    w,
    sent,
    attended,
    acc,
    partial,
    arrived,
    lists,
    place,
    hidden,
    span,
    list_sem,
    text_sem,
    in_sem,
    halo_sem,
    edge_sem,
    back_sem,
    out_sem,
    local_sem,
):
    me = lax.axis_index("seq")
    head = lax.axis_index("head")
    rows, width = q_hbm.shape
    heads = width // HD
    G = group_of(n_seq, heads)
    groups = n_seq // G
    chunks = heads // G
    trows = tk_hbm.shape[0]
    tw = chunks * HD
    reach_text = MOST - 1
    span_text = -(-MOST * trows // HD) * HD
    entries = near_ref.shape[1]
    out_rows = rows // n_head
    wide = w_hbm.shape[1]
    j = lax.rem(me, G)
    mine = me // G
    base = me - j

    if G == PLANE:
        jx, jy = lax.rem(j, 2), j // 2
        member = [j, 2 * jy + 1 - jx, 2 * (1 - jy) + jx, G - 1 - j]
    else:
        member = [j]
    peers = range(1, G)
    across_first = [3, 1, 2] if G == PLANE else []

    def part(i, size):
        return pl.ds(pl.multiple_of(i * size, HD), size)

    def push(src, dst, sem, at, to):
        return pltpu.make_async_remote_copy(
            src_ref=src,
            dst_ref=dst,
            send_sem=sem[0].at[at],
            recv_sem=sem[1].at[at],
            device_id=to,
            device_id_type=MESH,
        )

    def to_member(r):
        return {"seq": base + member[r]}

    def group_exists(by):
        return (mine + by >= 0) & (mine + by < groups)

    def list_copy(r):
        return push(near_ref, lists.at[j], list_sem, (r - 1,), to_member(r))

    def text_copy(r, s):
        src = (tk_hbm, tv_hbm)[s].at[:, part(member[r], tw)]
        dst = (tk, tv)[s].at[reach_text + j]
        return push(src, dst, text_sem, (r - 1, s), to_member(r))

    def in_copy(c, r, s):
        src = (k_hbm, v_hbm, q_hbm)[s].at[:, part(member[r] * chunks + c, HD)]
        dst = (k, v, q)[s][c].at[j if s == 2 else REACH + j]
        return push(src, dst, in_sem, (c, r - 1, s), to_member(r))

    hops = -(-REACH // G)
    text_hops = -(-reach_text // G)

    def halo_copy(c, by, i, s):
        src = (k, v)[s][c].at[REACH + i]
        slot = REACH + i - by * G
        dst = (k, v)[s][c].at[slot]
        n = slot if by > 0 else slot - REACH - G
        side = 0 if by > 0 else 1
        return push(src, dst, halo_sem, (c, side, n, s), {"seq": me + by * G})

    def halo_wanted(by, i):
        if by > 0:
            return by * G - i <= REACH
        return i - by * G - (G - 1) <= REACH

    def edge_copy(by, s):
        if by > 0:
            first = max(0, by * G - reach_text)
            count = G - first
        else:
            first = 0
            count = min(G, reach_text + by * G + G)
        src = (tk, tv)[s].at[pl.ds(reach_text + first, count)]
        dst = (tk, tv)[s].at[pl.ds(reach_text + first - by * G, count)]
        side = 0 if by > 0 else 1
        return push(src, dst, edge_sem, (side, abs(by) - 1, s), {"seq": me + by * G})

    def back_copy(c, r, p):
        block = lax.rem(head + 1 + p, n_head)
        at = pl.multiple_of(block * out_rows, out_rows)
        src = sent[c].at[member[r], pl.ds(at, out_rows)]
        dst = attended[c].at[pl.ds(at, out_rows), part(j, HD)]
        return push(src, dst, back_sem, (c, r - 1, p), to_member(r))

    def out_copy(d):
        peer = lax.rem(head + d, n_head)
        return push(partial.at[d - 1], arrived.at[d - 1], out_sem, (d - 1,), {"head": peer})

    own = []
    for c in range(chunks):
        for s, (hbm, buf) in enumerate(((k_hbm, k), (v_hbm, v), (q_hbm, q))):
            at = j if s == 2 else REACH + j
            own.append(
                pltpu.make_async_copy(
                    hbm.at[:, part(j * chunks + c, HD)], buf[c].at[at], local_sem.at[3 * c + s]
                )
            )
    own_text = [
        pltpu.make_async_copy(
            hbm.at[:, part(j, tw)], buf.at[reach_text + j], local_sem.at[3 * chunks + s]
        )
        for s, (hbm, buf) in enumerate(((tk_hbm, tk), (tv_hbm, tv)))
    ]
    weights = [
        pltpu.make_async_copy(
            w_hbm.at[pl.ds((i * chunks + c) * HD, HD)],
            w.at[c, pl.ds(i * HD, HD)],
            local_sem.at[3 * chunks + 2 + c * G + i],
        )
        for c in range(chunks)
        for i in range(G)
    ]

    for copy in own:
        copy.start()
    tk[...] = jnp.zeros_like(tk)
    tv[...] = jnp.zeros_like(tv)
    for copy in own_text:
        copy.start()
    for e in range(entries):
        lists[j, 0, e] = near_ref[0, e]

    barrier = pltpu.get_barrier_semaphore()
    partners = jnp.int32(n_head - 1 + G - 1)
    for r in peers:
        pl.semaphore_signal(barrier, inc=1, device_id=to_member(r), device_id_type=MESH)
    for d in range(1, n_head):
        peer = lax.rem(head + d, n_head)
        pl.semaphore_signal(barrier, inc=1, device_id={"head": peer}, device_id_type=MESH)
    for step in range(1, max(hops, text_hops) + 1):
        for by in (step, -step):
            partners = partners + group_exists(by).astype(jnp.int32)

            @pl.when(group_exists(by))
            def _():
                pl.semaphore_signal(
                    barrier, inc=1, device_id={"seq": me + by * G}, device_id_type=MESH
                )

    for copy in own + own_text:
        copy.wait()
    pl.semaphore_wait(barrier, partners)

    def send_in(c, kinds):
        for s in kinds:
            for r in across_first:
                in_copy(c, r, s).start()

    def forward(c, r, s):
        i = member[r]
        for step in range(1, hops + 1):
            for by in (step, -step):

                @pl.when(group_exists(by) & halo_wanted(by, i))
                def _():
                    halo_copy(c, by, i, s).start()

    def take(c, s):
        for r in (1, 2, 3) if G == PLANE else ():
            in_copy(c, r, s).wait_recv()
            forward(c, r, s)

    def halo_each(act):
        for step in range(1, hops + 1):
            for by in (step, -step):
                for i in range(G):
                    if halo_wanted(by, i):
                        act(by, i)

    def halo_arrive(c):
        def one(by, i):
            @pl.when(group_exists(-by))
            def _():
                for s in range(2):
                    halo_copy(c, by, i, s).wait_recv()

        halo_each(one)

    def halo_done(c):
        def one(by, i):
            @pl.when(group_exists(by))
            def _():
                for s in range(2):
                    halo_copy(c, by, i, s).wait_send()

        halo_each(one)

    def edge_each(act):
        for step in range(1, text_hops + 1):
            for by in (step, -step):
                act(by)

    for r in peers:
        list_copy(r).start()
    send_in(0, (0, 1))
    for r in across_first:
        for s in range(2):
            text_copy(r, s).start()
    send_in(0, (2,))
    for c in range(1, chunks):
        send_in(c, (0, 1))
    for c in range(1, chunks):
        send_in(c, (2,))
    for s in range(2):
        forward(0, 0, s)
    for copy in weights:
        copy.start()

    take(0, 0)
    take(0, 1)
    for r in peers:
        for s in range(2):
            text_copy(r, s).wait_recv()

    def edge_start(by):
        @pl.when(group_exists(by))
        def _():
            for s in range(2):
                edge_copy(by, s).start()

    edge_each(edge_start)
    for r in peers:
        list_copy(r).wait_recv()

    for i in range(G):
        tile = base + i
        found = []
        for e in range(entries):
            entry = lists[i, 0, e]
            good = entry >= 0
            for before in found:
                good = good & (entry != before)
            found.append(entry)
            good = good.astype(jnp.int32)
            slot = REACH + i + good * (entry - tile)
            place[i, e] = jnp.maximum(jnp.minimum(slot, G + 2 * REACH - 1), 0)
            hidden[i, e] = (1.0 - good.astype(jnp.float32)) * LOW
        start = jnp.int32(0)
        first_tile = jnp.int32(0)
        count = jnp.int32(0)
        for c in range(clip_ref.shape[0]):
            length = clip_ref[c]
            inside = ((start <= tile) & (tile < start + length)).astype(jnp.int32)
            first_tile = first_tile + inside * start
            count = count + inside * text_ref[c]
            start = start + length
        span[i, 0] = jnp.maximum(jnp.minimum(first_tile - base, G - 1) + reach_text, 0)
        span[i, 1] = count

    scale = HD ** (-0.5) * 1.4426950408889634
    column = lax.broadcasted_iota(jnp.int32, (1, span_text), 1)

    def fold(s):
        m = s[:, :HD]
        for n in range(1, s.shape[1] // HD):
            m = jnp.maximum(m, s[:, n * HD : (n + 1) * HD])
        return m

    def dot_t(a, b):
        return lax.dot_general(a, b, (((1,), (1,)), ((), ())), preferred_element_type=jnp.float32)

    def attend(c, r, p):
        i = member[r]
        block = lax.rem(head + 1 + p, n_head)
        at = pl.multiple_of(block * out_rows, out_rows)
        here = pl.ds(at, out_rows)
        q_part = q[c][i, here, :]
        slots = [place[i, e] for e in range(entries)]
        off = [hidden[i, e] for e in range(entries)]
        text_at = span[i, 0]

        def text_of(buf):
            runs = [buf[text_at + n, :, c * HD : (c + 1) * HD] for n in range(span_text // trows)]
            return jnp.concatenate(runs, axis=0)

        scores = [dot_t(q_part, k[c][slots[e]]) for e in range(entries)]
        text_score = dot_t(q_part, text_of(tk))
        text_score = text_score + jnp.where(column < span[i, 1], 0.0, -LOW)
        top = fold(text_score)
        for e in range(entries):
            top = jnp.maximum(top, fold(scores[e]) - off[e])
        top = jnp.max(top, axis=1, keepdims=True)
        ones = jnp.ones((rows, HD), jnp.bfloat16)
        text_ones = jnp.ones((span_text, HD), jnp.bfloat16)
        weight = jnp.exp2((text_score - top) * scale).astype(jnp.bfloat16)
        value = jnp.concatenate([text_of(tv), text_ones], axis=1)
        total = jnp.dot(weight, value, preferred_element_type=jnp.float32)
        for e in range(entries):
            weight = jnp.exp2((scores[e] - (top + off[e])) * scale).astype(jnp.bfloat16)
            value = jnp.concatenate([v[c][slots[e]], ones], axis=1)
            total = total + jnp.dot(weight, value, preferred_element_type=jnp.float32)
        result = (total[:, :HD] / total[:, HD:]).astype(jnp.bfloat16)
        if r == 0:
            attended[c][pl.ds(at, out_rows), part(j, HD)] = result
        else:
            sent[c][i, here, :] = result
            back_copy(c, r, p).start()

    order = across_first + [0]

    def compute(c, p, r):
        attend(c, r, p)

    def back_arrive(c, p):
        for r in peers:
            back_copy(c, r, p).wait_recv()

    parts = 6 if wide % (6 * HD) == 0 else 1
    pw = wide // parts

    def project(c):
        def one(n, carry):
            cols = part(n, pw)
            add = jnp.dot(attended[c][...], w[c, :, cols], preferred_element_type=jnp.float32)
            if c == 0:
                acc[:, cols] = add
            else:
                acc[:, cols] = acc[:, cols] + add
            return carry

        lax.fori_loop(0, parts, one, 0)

    def project_last(c, p):
        block = lax.rem(head + 1 + p, n_head)
        at = pl.ds(pl.multiple_of(block * out_rows, out_rows), out_rows)

        def one(n, carry):
            cols = part(n, pw)
            add = jnp.dot(attended[c][at, :], w[c, :, cols], preferred_element_type=jnp.float32)
            if chunks > 1:
                add = add + acc[at, cols]
            add = add.astype(jnp.bfloat16)
            if p < n_head - 1:
                partial[p, :, cols] = add
            else:
                add = add.astype(jnp.float32)
                for d in range(1, n_head):
                    add = add + arrived[d - 1, :, cols].astype(jnp.float32)
                out_ref[:, cols] = add.astype(jnp.bfloat16)
            return carry

        if p == n_head - 1:
            for d in range(1, n_head):
                out_copy(d).wait_recv()
        lax.fori_loop(0, parts, one, 0)
        if p < n_head - 1:
            out_copy(p + 1).start()

    pending = []
    for c in range(1, chunks):
        pending.append(lambda c=c: [forward(c, 0, s) for s in range(2)])
        for s in range(2):
            pending.append(lambda c=c, s=s: take(c, s))
    if chunks > 1:
        for _ in range(3):
            pending.pop(0)()
    def edge_arrive(by):
        @pl.when(group_exists(-by))
        def _():
            for s in range(2):
                edge_copy(by, s).wait_recv()

    edge_each(edge_arrive)
    for c in range(chunks):
        for r in peers:
            in_copy(c, r, 2).wait_recv()
        halo_arrive(c)
        for p in range(n_head):
            for r in order:
                compute(c, p, r)
                if pending:
                    pending.pop(0)()
    for act in pending:
        act()
    for copy in weights:
        copy.wait()
    for c in range(chunks - 1):
        for p in range(n_head):
            back_arrive(c, p)
        project(c)
    for p in range(n_head):
        back_arrive(chunks - 1, p)
        project_last(chunks - 1, p)

    for r in peers:
        list_copy(r).wait_send()
        for s in range(2):
            text_copy(r, s).wait_send()
        for c in range(chunks):
            for s in range(3):
                in_copy(c, r, s).wait_send()
            for p in range(n_head):
                back_copy(c, r, p).wait_send()
    for c in range(chunks):
        halo_done(c)

    def edge_done(by):
        @pl.when(group_exists(by))
        def _():
            for s in range(2):
                edge_copy(by, s).wait_send()

    edge_each(edge_done)
    for d in range(1, n_head):
        out_copy(d).wait_send()


def body(n_seq, n_head, q, k, v, tk, tv, near, clip_lengths, text_lengths, w):
    rows, width = q.shape
    heads = width // HD
    G = group_of(n_seq, heads)
    chunks = heads // G
    wide = w.shape[1]
    out_rows = rows // n_head
    trows = tk.shape[0]
    span_text = -(-MOST * trows // HD) * HD
    slots = G + 2 * REACH
    hops = -(-REACH // G)
    text_hops = -(-(MOST - 1) // G)
    others = max(G - 1, 1)
    window = max(G + 2 * (MOST - 1), G + MOST - 2 + span_text // trows)
    smem = pl.BlockSpec(memory_space=pltpu.SMEM)
    hbm = pl.BlockSpec(memory_space=pl.ANY)
    bf16, f32 = jnp.bfloat16, jnp.float32

    def pair(*shape):
        return [pltpu.SemaphoreType.DMA(shape), pltpu.SemaphoreType.DMA(shape)]

    return pl.pallas_call(
        functools.partial(kernel, n_seq, n_head),
        out_shape=jax.ShapeDtypeStruct((out_rows, wide), bf16),
        in_specs=[smem] * 3 + [hbm] * 6,
        out_specs=pl.BlockSpec(memory_space=pltpu.VMEM),
        scratch_shapes=[
            [pltpu.VMEM((G, rows, HD), bf16) for _ in range(chunks)],
            [pltpu.VMEM((slots, rows, HD), bf16) for _ in range(chunks)],
            [pltpu.VMEM((slots, rows, HD), bf16) for _ in range(chunks)],
            pltpu.VMEM((window, trows, chunks * HD), bf16),
            pltpu.VMEM((window, trows, chunks * HD), bf16),
            pltpu.VMEM((chunks, G * HD, wide), bf16),
            [pltpu.VMEM((G, rows, HD), bf16) for _ in range(chunks)],
            [pltpu.VMEM((rows, G * HD), bf16) for _ in range(chunks)],
            pltpu.VMEM((rows, wide), f32),
            pltpu.VMEM((n_head - 1, out_rows, wide), bf16),
            pltpu.VMEM((n_head - 1, out_rows, wide), bf16),
            pltpu.SMEM((G,) + near.shape, jnp.int32),
            pltpu.SMEM((G, near.shape[1]), jnp.int32),
            pltpu.SMEM((G, near.shape[1]), f32),
            pltpu.SMEM((G, 2), jnp.int32),
            pair(others),
            pair(others, 2),
            pair(chunks, others, 3),
            pair(chunks, 2, REACH, 2),
            pair(2, text_hops, 2),
            pair(chunks, others, n_head),
            pair(n_head - 1),
            pltpu.SemaphoreType.DMA((3 * chunks + 2 + chunks * G,)),
        ],
        compiler_params=pltpu.CompilerParams(
            collective_id=0, has_side_effects=True, vmem_limit_bytes=58 << 20
        ),
    )(near, clip_lengths, text_lengths, q, k, v, tk, tv, w)


def solution(mesh):
    placed = (
        P("seq", "head"),
        P("seq", "head"),
        P("seq", "head"),
        P("seq", "head"),
        P("seq", "head"),
        P("seq", None),
        P(),
        P(),
        P("head", None),
    )
    return jax.shard_map(
        functools.partial(body, mesh.shape["seq"], mesh.shape["head"]),
        mesh=mesh,
        in_specs=placed,
        out_specs=P(("seq", "head"), None),
        check_vma=False,
    )
```

```python
import functools

import jax
import jax.numpy as jnp
from jax import lax
from jax.experimental import pallas as pl
from jax.experimental.pallas import tpu as pltpu
from jax.sharding import PartitionSpec as P

HD = 128
REACH = 3
MOST = 7
PLANE = 4
LOW = 1e30
MESH = pl.DeviceIdType.MESH


def group_of(n_seq, heads):
    return PLANE if n_seq % PLANE == 0 and heads % PLANE == 0 else 1


def kernel(
    n_seq,
    n_head,
    near_ref,
    clip_ref,
    text_ref,
    q_hbm,
    k_hbm,
    v_hbm,
    tk_hbm,
    tv_hbm,
    w_hbm,
    out_ref,
    q,
    k,
    v,
    tk,
    tv,
    w,
    sent,
    attended,
    acc,
    partial,
    arrived,
    lists,
    place,
    hidden,
    span,
    list_sem,
    text_sem,
    in_sem,
    halo_sem,
    edge_sem,
    chain_sem,
    back_sem,
    out_sem,
    local_sem,
):
    me = lax.axis_index("seq")
    head = lax.axis_index("head")
    rows, width = q_hbm.shape
    heads = width // HD
    G = group_of(n_seq, heads)
    groups = n_seq // G
    chunks = heads // G
    trows = tk_hbm.shape[0]
    tw = chunks * HD
    reach_text = MOST - 1
    span_text = -(-MOST * trows // HD) * HD
    entries = near_ref.shape[1]
    out_rows = rows // n_head
    wide = w_hbm.shape[1]
    j = lax.rem(me, G)
    mine = me // G
    base = me - j

    jx, jy = lax.rem(j, 2), j // 2

    def member(r):
        return 2 * lax.rem(jy + r // 2, 2) + lax.rem(jx + lax.rem(r, 2), 2) if G == PLANE else j

    peers = range(1, G)

    def part(i, size):
        return pl.ds(pl.multiple_of(i * size, HD), size)

    def push(src, dst, sem, at, to):
        return pltpu.make_async_remote_copy(
            src_ref=src,
            dst_ref=dst,
            send_sem=sem[0].at[at],
            recv_sem=sem[1].at[at],
            device_id=to,
            device_id_type=MESH,
        )

    def to_member(r):
        return {"seq": base + member(r)}

    def group_exists(by):
        return (mine + by >= 0) & (mine + by < groups)

    def list_copy(r):
        return push(near_ref, lists.at[j], list_sem, (r - 1,), to_member(r))

    def text_copy(r, s):
        src = (tk_hbm, tv_hbm)[s].at[:, part(member(r), tw)]
        dst = (tk, tv)[s].at[reach_text + j]
        return push(src, dst, text_sem, (r - 1, s), to_member(r))

    def in_copy(c, r, s):
        src = (k_hbm, v_hbm, q_hbm)[s].at[:, part(member(r) * chunks + c, HD)]
        dst = (k, v, q)[s][c].at[j if s == 2 else REACH + j]
        return push(src, dst, in_sem, (c, r - 1, s), to_member(r))

    hops = -(-REACH // G)
    chained = G < reach_text <= 2 * G
    text_hops = 1 if chained else -(-reach_text // G)

    def halo_copy(c, by, i, s):
        src = (k, v)[s][c].at[REACH + i]
        slot = REACH + i - by * G
        dst = (k, v)[s][c].at[slot]
        n = slot if by > 0 else slot - REACH - G
        side = 0 if by > 0 else 1
        return push(src, dst, halo_sem, (c, side, n, s), {"seq": me + by * G})

    def halo_wanted(by, i):
        if by > 0:
            return by * G - i <= REACH
        return i - by * G - (G - 1) <= REACH

    def edge_copy(by, s):
        if by > 0:
            first = max(0, by * G - reach_text)
            count = G - first
        else:
            first = 0
            count = min(G, reach_text + by * G + G)
        src = (tk, tv)[s].at[pl.ds(reach_text + first, count)]
        dst = (tk, tv)[s].at[pl.ds(reach_text + first - by * G, count)]
        side = 0 if by > 0 else 1
        return push(src, dst, edge_sem, (side, abs(by) - 1, s), {"seq": me + by * G})

    def chain_copy(by, s):
        count = reach_text - G
        first = G if by > 0 else reach_text + G
        src = (tk, tv)[s].at[pl.ds(first, count)]
        dst = (tk, tv)[s].at[pl.ds(first - by * G, count)]
        return push(src, dst, chain_sem, (0 if by > 0 else 1, s), {"seq": me + by * G})

    def back_copy(c, r, p):
        block = lax.rem(head + 1 + p, n_head)
        at = pl.multiple_of(block * out_rows, out_rows)
        src = sent[c].at[member(r), pl.ds(at, out_rows)]
        dst = attended[c].at[pl.ds(at, out_rows), part(j, HD)]
        return push(src, dst, back_sem, (c, r - 1, p), to_member(r))

    def out_copy(d):
        peer = lax.rem(head + d, n_head)
        return push(partial.at[d - 1], arrived.at[d - 1], out_sem, (d - 1,), {"head": peer})

    own = []
    for c in range(chunks):
        for s, (hbm, buf) in enumerate(((k_hbm, k), (v_hbm, v), (q_hbm, q))):
            at = j if s == 2 else REACH + j
            own.append(
                pltpu.make_async_copy(
                    hbm.at[:, part(j * chunks + c, HD)], buf[c].at[at], local_sem.at[3 * c + s]
                )
            )
    own_text = [
        pltpu.make_async_copy(
            hbm.at[:, part(j, tw)], buf.at[reach_text + j], local_sem.at[3 * chunks + s]
        )
        for s, (hbm, buf) in enumerate(((tk_hbm, tk), (tv_hbm, tv)))
    ]
    weights = [
        pltpu.make_async_copy(
            w_hbm.at[pl.ds((i * chunks + c) * HD, HD)],
            w.at[c, pl.ds(i * HD, HD)],
            local_sem.at[3 * chunks + 2 + c * G + i],
        )
        for c in range(chunks)
        for i in range(G)
    ]

    for copy in own:
        copy.start()
    tk[...] = jnp.zeros_like(tk)
    tv[...] = jnp.zeros_like(tv)
    for copy in own_text:
        copy.start()
    for e in range(entries):
        lists[j, 0, e] = near_ref[0, e]

    barrier = pltpu.get_barrier_semaphore()
    partners = jnp.int32(n_head - 1 + G - 1)
    for r in peers:
        pl.semaphore_signal(barrier, inc=1, device_id=to_member(r), device_id_type=MESH)
    for d in range(1, n_head):
        peer = lax.rem(head + d, n_head)
        pl.semaphore_signal(barrier, inc=1, device_id={"head": peer}, device_id_type=MESH)
    for step in range(1, max(hops, text_hops) + 1):
        for by in (step, -step):
            partners = partners + group_exists(by).astype(jnp.int32)

            @pl.when(group_exists(by))
            def _():
                pl.semaphore_signal(
                    barrier, inc=1, device_id={"seq": me + by * G}, device_id_type=MESH
                )

    for copy in own + own_text:
        copy.wait()
    pl.semaphore_wait(barrier, partners)

    def send_in(c, kinds):
        for s in kinds:
            for r in peers:
                in_copy(c, r, s).start()

    def forward(c, r, s):
        i = member(r)
        for step in range(1, hops + 1):
            for by in (step, -step):

                @pl.when(group_exists(by) & halo_wanted(by, i))
                def _():
                    halo_copy(c, by, i, s).start()

    def take(c, s):
        for r in peers:
            in_copy(c, r, s).wait_recv()
            forward(c, r, s)

    def halo_each(act):
        for step in range(1, hops + 1):
            for by in (step, -step):
                for i in range(G):
                    if halo_wanted(by, i):
                        act(by, i)

    def halo_arrive(c):
        def one(by, i):
            @pl.when(group_exists(-by))
            def _():
                for s in range(2):
                    halo_copy(c, by, i, s).wait_recv()

        halo_each(one)

    def halo_done(c):
        def one(by, i):
            @pl.when(group_exists(by))
            def _():
                for s in range(2):
                    halo_copy(c, by, i, s).wait_send()

        halo_each(one)

    def edge_each(act):
        for step in range(1, text_hops + 1):
            for by in (step, -step):
                act(by)

    for r in peers:
        list_copy(r).start()
    send_in(0, (0, 1))
    for r in peers:
        for s in range(2):
            text_copy(r, s).start()
    send_in(0, (2,))
    for c in range(1, chunks):
        send_in(c, (0, 1))
    for c in range(1, chunks):
        send_in(c, (2,))
    for s in range(2):
        forward(0, 0, s)
    for copy in weights:
        copy.start()

    take(0, 0)
    take(0, 1)
    for r in peers:
        for s in range(2):
            text_copy(r, s).wait_recv()

    def edge_start(by):
        @pl.when(group_exists(by))
        def _():
            for s in range(2):
                edge_copy(by, s).start()

    edge_each(edge_start)
    for r in peers:
        list_copy(r).wait_recv()

    for i in range(G):
        tile = base + i
        found = []
        for e in range(entries):
            entry = lists[i, 0, e]
            good = entry >= 0
            for before in found:
                good = good & (entry != before)
            found.append(entry)
            good = good.astype(jnp.int32)
            slot = REACH + i + good * (entry - tile)
            place[i, e] = jnp.maximum(jnp.minimum(slot, G + 2 * REACH - 1), 0)
            hidden[i, e] = (1.0 - good.astype(jnp.float32)) * LOW
        start = jnp.int32(0)
        first_tile = jnp.int32(0)
        count = jnp.int32(0)
        for c in range(clip_ref.shape[0]):
            length = clip_ref[c]
            inside = ((start <= tile) & (tile < start + length)).astype(jnp.int32)
            first_tile = first_tile + inside * start
            count = count + inside * text_ref[c]
            start = start + length
        span[i, 0] = jnp.maximum(jnp.minimum(first_tile - base, G - 1) + reach_text, 0)
        span[i, 1] = count

    scale = HD ** (-0.5) * 1.4426950408889634
    column = lax.broadcasted_iota(jnp.int32, (1, span_text), 1)

    def fold(s, pick):
        m = s[:, :HD]
        for n in range(1, s.shape[1] // HD):
            m = pick(m, s[:, n * HD : (n + 1) * HD])
        return m

    def dot_t(a, b):
        return lax.dot_general(a, b, (((1,), (1,)), ((), ())), preferred_element_type=jnp.float32)

    def attend(c, r):
        i = member(r)
        q_part = q[c][i]
        slots = [place[i, e] for e in range(entries)]
        off = [hidden[i, e] for e in range(entries)]
        text_at = span[i, 0]

        def text_of(buf):
            runs = [buf[text_at + n, :, c * HD : (c + 1) * HD] for n in range(span_text // trows)]
            return jnp.concatenate(runs, axis=0)

        scores = [dot_t(q_part, k[c][slots[e]]) for e in range(entries)]
        text_score = dot_t(q_part, text_of(tk))
        text_score = text_score + jnp.where(column < span[i, 1], 0.0, -LOW)
        top = fold(text_score, jnp.maximum)
        for e in range(entries):
            top = jnp.maximum(top, fold(scores[e], jnp.maximum) - off[e])
        top = jnp.max(top, axis=1, keepdims=True)
        weight = jnp.exp2((text_score - top) * scale)
        total = fold(weight, jnp.add)
        result = jnp.dot(
            weight.astype(jnp.bfloat16), text_of(tv), preferred_element_type=jnp.float32
        )
        for e in range(entries):
            weight = jnp.exp2((scores[e] - (top + off[e])) * scale)
            total = total + fold(weight, jnp.add)
            result = result + jnp.dot(
                weight.astype(jnp.bfloat16), v[c][slots[e]], preferred_element_type=jnp.float32
            )
        result = result / jnp.sum(total, axis=1, keepdims=True)
        sent[c][i] = result.astype(jnp.bfloat16)
        if G > 1:

            @pl.when(r > 0)
            def _():
                for p in range(n_head):
                    back_copy(c, r, p).start()

    def compute(c):
        def one(n, carry):
            for at, act in enumerate(pending[c]):
                pl.when(n == at)(lambda act=act: act() and None)
            attend(c, G - 1 - n)
            return carry

        lax.fori_loop(0, G, one, 0)
        attended[c][:, part(j, HD)] = sent[c][j]

    def back_arrive(c, p):
        for r in peers:
            back_copy(c, r, p).wait_recv()

    parts = 6 if wide % (6 * HD) == 0 else 1
    pw = wide // parts

    def project(c):
        def one(n, carry):
            cols = part(n, pw)
            add = jnp.dot(attended[c][...], w[c, :, cols], preferred_element_type=jnp.float32)
            if c == 0:
                acc[:, cols] = add
            else:
                acc[:, cols] = acc[:, cols] + add
            return carry

        lax.fori_loop(0, parts, one, 0)

    def project_last(c, p):
        block = lax.rem(head + 1 + p, n_head)
        at = pl.ds(pl.multiple_of(block * out_rows, out_rows), out_rows)

        def one(n, carry):
            cols = part(n, pw)
            add = jnp.dot(attended[c][at, :], w[c, :, cols], preferred_element_type=jnp.float32)
            if chunks > 1:
                add = add + acc[at, cols]
            add = add.astype(jnp.bfloat16)
            if p < n_head - 1:
                partial[p, :, cols] = add
            else:
                add = add.astype(jnp.float32)
                for d in range(1, n_head):
                    add = add + arrived[d - 1, :, cols].astype(jnp.float32)
                out_ref[:, cols] = add.astype(jnp.bfloat16)
            return carry

        if p == n_head - 1:
            for d in range(1, n_head):
                out_copy(d).wait_recv()
        lax.fori_loop(0, parts, one, 0)
        if p < n_head - 1:
            out_copy(p + 1).start()

    def edge_arrive(by):
        @pl.when(group_exists(-by))
        def _():
            for s in range(2):
                edge_copy(by, s).wait_recv()

        if chained:

            @pl.when(group_exists(-by) & group_exists(by))
            def _():
                for s in range(2):
                    chain_copy(by, s).start()

    def chain_arrive(by):
        if chained:

            @pl.when(group_exists(-2 * by))
            def _():
                for s in range(2):
                    chain_copy(by, s).wait_recv()

    later = []
    for c in range(1, chunks):
        later.append(lambda c=c: [forward(c, 0, s) for s in range(2)])
        if c == 1:
            later.append(lambda: edge_each(edge_arrive))
        for s in range(2):
            later.append(lambda c=c, s=s: take(c, s))
    if chunks > 1:
        for act in later[:4]:
            act()
    else:
        edge_each(edge_arrive)
    edge_each(chain_arrive)
    pending = {c: later[4:] if c == 0 else [] for c in range(chunks)}

    def settle(c):
        for p in range(n_head):
            back_arrive(c, p)
        if c == 0:
            for copy in weights:
                copy.wait()
        project(c)

    for c in range(chunks):
        if 2 <= c:
            settle(c - 2)
        for r in peers:
            in_copy(c, r, 2).wait_recv()
        halo_arrive(c)
        compute(c)
    if chunks > 1:
        settle(chunks - 2)
    else:
        for copy in weights:
            copy.wait()
    for p in range(n_head):
        back_arrive(chunks - 1, p)
        project_last(chunks - 1, p)

    for r in peers:
        list_copy(r).wait_send()
        for s in range(2):
            text_copy(r, s).wait_send()
        for c in range(chunks):
            for s in range(3):
                in_copy(c, r, s).wait_send()
            for p in range(n_head):
                back_copy(c, r, p).wait_send()
    for c in range(chunks):
        halo_done(c)

    def edge_done(by):
        @pl.when(group_exists(by))
        def _():
            for s in range(2):
                edge_copy(by, s).wait_send()

        if chained:

            @pl.when(group_exists(-by) & group_exists(by))
            def _():
                for s in range(2):
                    chain_copy(by, s).wait_send()

    edge_each(edge_done)
    for d in range(1, n_head):
        out_copy(d).wait_send()


def body(n_seq, n_head, q, k, v, tk, tv, near, clip_lengths, text_lengths, w):
    rows, width = q.shape
    heads = width // HD
    G = group_of(n_seq, heads)
    chunks = heads // G
    wide = w.shape[1]
    out_rows = rows // n_head
    trows = tk.shape[0]
    span_text = -(-MOST * trows // HD) * HD
    slots = G + 2 * REACH
    hops = -(-REACH // G)
    text_hops = 1 if G < MOST - 1 <= 2 * G else -(-(MOST - 1) // G)
    others = max(G - 1, 1)
    window = max(G + 2 * (MOST - 1), G + MOST - 2 + span_text // trows)
    smem = pl.BlockSpec(memory_space=pltpu.SMEM)
    hbm = pl.BlockSpec(memory_space=pl.ANY)
    bf16, f32 = jnp.bfloat16, jnp.float32

    def pair(*shape):
        return [pltpu.SemaphoreType.DMA(shape), pltpu.SemaphoreType.DMA(shape)]

    return pl.pallas_call(
        functools.partial(kernel, n_seq, n_head),
        out_shape=jax.ShapeDtypeStruct((out_rows, wide), bf16),
        in_specs=[smem] * 3 + [hbm] * 6,
        out_specs=pl.BlockSpec(memory_space=pltpu.VMEM),
        scratch_shapes=[
            [pltpu.VMEM((G, rows, HD), bf16) for _ in range(chunks)],
            [pltpu.VMEM((slots, rows, HD), bf16) for _ in range(chunks)],
            [pltpu.VMEM((slots, rows, HD), bf16) for _ in range(chunks)],
            pltpu.VMEM((window, trows, chunks * HD), bf16),
            pltpu.VMEM((window, trows, chunks * HD), bf16),
            pltpu.VMEM((chunks, G * HD, wide), bf16),
            [pltpu.VMEM((G, rows, HD), bf16) for _ in range(chunks)],
            [pltpu.VMEM((rows, G * HD), bf16) for _ in range(chunks)],
            pltpu.VMEM((rows, wide), f32),
            pltpu.VMEM((n_head - 1, out_rows, wide), bf16),
            pltpu.VMEM((n_head - 1, out_rows, wide), bf16),
            pltpu.SMEM((G,) + near.shape, jnp.int32),
            pltpu.SMEM((G, near.shape[1]), jnp.int32),
            pltpu.SMEM((G, near.shape[1]), f32),
            pltpu.SMEM((G, 2), jnp.int32),
            pair(others),
            pair(others, 2),
            pair(chunks, others, 3),
            pair(chunks, 2, REACH, 2),
            pair(2, text_hops, 2),
            pair(2, 2),
            pair(chunks, others, n_head),
            pair(n_head - 1),
            pltpu.SemaphoreType.DMA((3 * chunks + 2 + chunks * G,)),
        ],
        compiler_params=pltpu.CompilerParams(
            collective_id=0, has_side_effects=True, vmem_limit_bytes=58 << 20
        ),
    )(near, clip_lengths, text_lengths, q, k, v, tk, tv, w)


def solution(mesh):
    placed = (
        P("seq", "head"),
        P("seq", "head"),
        P("seq", "head"),
        P("seq", "head"),
        P("seq", "head"),
        P("seq", None),
        P(),
        P(),
        P("head", None),
    )
    return jax.shard_map(
        functools.partial(body, mesh.shape["seq"], mesh.shape["head"]),
        mesh=mesh,
        in_specs=placed,
        out_specs=P(("seq", "head"), None),
        check_vma=False,
    )
```

```python
import functools

import jax
import jax.numpy as jnp
from jax import lax
from jax.experimental import pallas as pl
from jax.experimental.pallas import tpu as pltpu
from jax.sharding import PartitionSpec as P

HD = 128
REACH = 3
MOST = 7
PLANE = 4
LOW = 1e30
MESH = pl.DeviceIdType.MESH


def group_of(n_seq, heads):
    return PLANE if n_seq % PLANE == 0 and heads % PLANE == 0 else 1


def kernel(
    n_seq,
    n_head,
    near_ref,
    clip_ref,
    text_ref,
    q_hbm,
    k_hbm,
    v_hbm,
    tk_hbm,
    tv_hbm,
    w_hbm,
    out_ref,
    q,
    k,
    v,
    far_k,
    far_v,
    tk,
    tv,
    w,
    top_a,
    total_a,
    acc_a,
    sent,
    attended,
    acc,
    mixed,
    lists,
    place,
    hidden,
    far_hidden,
    span,
    list_sem,
    text_sem,
    in_sem,
    halo_sem,
    edge_sem,
    chain_sem,
    back_sem,
    weight_sem,
    out_sem,
    local_sem,
):
    me = lax.axis_index("seq")
    head = lax.axis_index("head")
    rows, width = q_hbm.shape
    heads = width // HD
    G = group_of(n_seq, heads)
    groups = n_seq // G
    chunks = heads // G
    trows = tk_hbm.shape[0]
    tw = chunks * HD
    reach_text = MOST - 1
    span_text = -(-MOST * trows // HD) * HD
    entries = near_ref.shape[1]
    out_rows = rows // n_head
    wide = w_hbm.shape[1]
    j = lax.rem(me, G)
    mine = me // G
    base = me - j

    jx, jy = lax.rem(j, 2), j // 2

    def member(r):
        return 2 * lax.rem(jy + r // 2, 2) + lax.rem(jx + lax.rem(r, 2), 2) if G == PLANE else j

    peers = range(1, G)

    def part(i, size):
        return pl.ds(pl.multiple_of(i * size, HD), size)

    def push(src, dst, sem, at, to):
        return pltpu.make_async_remote_copy(
            src_ref=src,
            dst_ref=dst,
            send_sem=sem[0].at[at],
            recv_sem=sem[1].at[at],
            device_id=to,
            device_id_type=MESH,
        )

    def to_member(r):
        return {"seq": base + member(r)}

    def group_exists(by):
        return (mine + by >= 0) & (mine + by < groups)

    def list_copy(r):
        return push(near_ref, lists.at[j], list_sem, (r - 1,), to_member(r))

    def text_copy(r, s):
        src = (tk_hbm, tv_hbm)[s].at[:, part(member(r), tw)]
        dst = (tk, tv)[s].at[reach_text + j]
        return push(src, dst, text_sem, (r - 1, s), to_member(r))

    def in_copy(c, r, s):
        src = (k_hbm, v_hbm, q_hbm)[s].at[:, part(member(r) * chunks + c, HD)]
        dst = (k, v, q)[s][c].at[j]
        return push(src, dst, in_sem, (c, r - 1, s), to_member(r))

    around = 0 if groups == 1 else (2 if G == PLANE else entries - 1)
    hops = -(-REACH // G)
    chained = G < reach_text <= 2 * G
    text_hops = 1 if chained else -(-reach_text // G)

    def halo_copy(c, by, i, s):
        slot = REACH + i - by * G if by > 0 else REACH + i - by * G - G
        dst = (far_k, far_v)[s][c].at[slot]
        return push((k, v)[s][c].at[i], dst, halo_sem, (c, slot, s), {"seq": me + by * G})

    def halo_wanted(by, i):
        if by > 0:
            return by * G - i <= REACH
        return i - by * G - (G - 1) <= REACH

    def edge_copy(by, s):
        if by > 0:
            first = max(0, by * G - reach_text)
            count = G - first
        else:
            first = 0
            count = min(G, reach_text + by * G + G)
        src = (tk, tv)[s].at[pl.ds(reach_text + first, count)]
        dst = (tk, tv)[s].at[pl.ds(reach_text + first - by * G, count)]
        side = 0 if by > 0 else 1
        return push(src, dst, edge_sem, (side, abs(by) - 1, s), {"seq": me + by * G})

    def chain_copy(by, s):
        count = reach_text - G
        first = G if by > 0 else reach_text + G
        src = (tk, tv)[s].at[pl.ds(first, count)]
        dst = (tk, tv)[s].at[pl.ds(first - by * G, count)]
        return push(src, dst, chain_sem, (0 if by > 0 else 1, s), {"seq": me + by * G})

    def back_copy(c, r, d):
        to = lax.rem(head + d, n_head)
        src = sent[c].at[member(r), pl.ds(pl.multiple_of(to * out_rows, out_rows), out_rows)]
        dst = attended[c].at[:, part(j * n_head + head, HD)]
        return push(src, dst, back_sem, (c, r, d), {"seq": base + member(r), "head": to})

    def weight_copy(c, i, d):
        src = w_hbm.at[pl.ds((i * chunks + c) * HD, HD)]
        at = pl.ds(pl.multiple_of((i * n_head + head) * HD, HD), HD)
        if d == 0:
            return pltpu.make_async_copy(src, w.at[c, at], local_sem.at[3 * chunks + 2 + c * G + i])
        to = lax.rem(head + d, n_head)
        return push(src, w.at[c, at], weight_sem, (c * G + i, d - 1), {"head": to})

    def weight_each(act):
        for c in range(chunks):
            for i in range(G):
                for d in range(n_head):
                    act(c, i, d)

    own = []
    for c in range(chunks):
        for s, (hbm, buf) in enumerate(((k_hbm, k), (v_hbm, v), (q_hbm, q))):
            own.append(
                pltpu.make_async_copy(
                    hbm.at[:, part(j * chunks + c, HD)], buf[c].at[j], local_sem.at[3 * c + s]
                )
            )
    own_text = [
        pltpu.make_async_copy(
            hbm.at[:, part(j, tw)], buf.at[reach_text + j], local_sem.at[3 * chunks + s]
        )
        for s, (hbm, buf) in enumerate(((tk_hbm, tk), (tv_hbm, tv)))
    ]
    for copy in own:
        copy.start()
    tk[...] = jnp.zeros_like(tk)
    tv[...] = jnp.zeros_like(tv)
    for copy in own_text:
        copy.start()
    for e in range(entries):
        lists[j, 0, e] = near_ref[0, e]

    barrier = pltpu.get_barrier_semaphore()
    partners = jnp.int32(n_head * G - 1)
    for r in range(G):
        for d in range(n_head):
            if r + d > 0:
                to = {"seq": base + member(r), "head": lax.rem(head + d, n_head)}
                pl.semaphore_signal(barrier, inc=1, device_id=to, device_id_type=MESH)
    for step in range(1, max(hops, text_hops) + 1):
        for by in (step, -step):
            partners = partners + group_exists(by).astype(jnp.int32)

            @pl.when(group_exists(by))
            def _():
                pl.semaphore_signal(
                    barrier, inc=1, device_id={"seq": me + by * G}, device_id_type=MESH
                )

    for copy in own + own_text:
        copy.wait()
    pl.semaphore_wait(barrier, partners)

    def send_in(c, kinds):
        for s in kinds:
            for r in peers:
                in_copy(c, r, s).start()

    def forward(c, r, s):
        i = member(r)
        for step in range(1, hops + 1):
            for by in (step, -step):

                @pl.when(group_exists(by) & halo_wanted(by, i))
                def _():
                    halo_copy(c, by, i, s).start()

    def take(c, s):
        for r in peers:
            in_copy(c, r, s).wait_recv()
            forward(c, r, s)

    def halo_each(act):
        for step in range(1, hops + 1):
            for by in (step, -step):
                for i in range(G):
                    if halo_wanted(by, i):
                        act(by, i)

    def halo_arrive(c):
        def one(by, i):
            @pl.when(group_exists(-by))
            def _():
                for s in range(2):
                    halo_copy(c, by, i, s).wait_recv()

        halo_each(one)

    def halo_done(c):
        def one(by, i):
            @pl.when(group_exists(by))
            def _():
                for s in range(2):
                    halo_copy(c, by, i, s).wait_send()

        halo_each(one)

    def edge_each(act):
        for step in range(1, text_hops + 1):
            for by in (step, -step):
                act(by)

    for r in peers:
        list_copy(r).start()
    for s in range(2):
        for r in peers:
            text_copy(r, s).start()
    for c in range(chunks):
        send_in(c, (0, 1, 2))
    for s in range(2):
        forward(0, 0, s)
    weight_each(lambda c, i, d: weight_copy(c, i, d).start())

    def edge_start(by):
        @pl.when(group_exists(by))
        def _():
            for s in range(2):
                edge_copy(by, s).start()

    def edge_arrive(by):
        @pl.when(group_exists(-by))
        def _():
            for s in range(2):
                edge_copy(by, s).wait_recv()

        if chained:

            @pl.when(group_exists(-by) & group_exists(by))
            def _():
                for s in range(2):
                    chain_copy(by, s).start()

    def chain_arrive(by):
        if chained:

            @pl.when(group_exists(-2 * by))
            def _():
                for s in range(2):
                    chain_copy(by, s).wait_recv()

    for r in peers:
        for s in range(2):
            text_copy(r, s).wait_recv()
    edge_each(edge_start)
    take(0, 0)
    edge_each(edge_arrive)
    take(0, 1)
    if chunks > 1:
        for s in range(2):
            forward(1, 0, s)
    for r in peers:
        list_copy(r).wait_recv()

    spare = REACH - group_exists(-1).astype(jnp.int32)
    for i in range(G):
        tile = base + i
        for t in range(G):
            listed = lists[i, 0, 0] == base + t
            for e in range(1, entries):
                listed = listed | (lists[i, 0, e] == base + t)
            hidden[i, t] = (1.0 - listed.astype(jnp.float32)) * LOW
        slots = [jnp.int32(0) for _ in range(around)]
        count = jnp.int32(0)
        for e in range(entries):
            entry = lists[i, 0, e]
            rel = entry - base
            outside = (entry >= 0) & ((rel < 0) | (rel >= G))
            for before in range(e):
                outside = outside & (entry != lists[i, 0, before])
            outside = outside.astype(jnp.int32)
            slot = rel + REACH - G * (rel >= G).astype(jnp.int32)
            for n in range(around):
                slots[n] = slots[n] + outside * (count == n).astype(jnp.int32) * slot
            count = count + outside
        for n in range(around):
            used = (n < count).astype(jnp.int32)
            slot = used * slots[n] + (1 - used) * spare
            place[i, n] = jnp.maximum(jnp.minimum(slot, 2 * REACH - 1), 0)
            far_hidden[i, n] = (1.0 - used.astype(jnp.float32)) * LOW
        start = jnp.int32(0)
        first_tile = jnp.int32(0)
        count = jnp.int32(0)
        for c in range(clip_ref.shape[0]):
            length = clip_ref[c]
            inside = ((start <= tile) & (tile < start + length)).astype(jnp.int32)
            first_tile = first_tile + inside * start
            count = count + inside * text_ref[c]
            start = start + length
        span[i, 0] = jnp.maximum(jnp.minimum(first_tile - base, G - 1) + reach_text, 0)
        span[i, 1] = count

    scale = HD ** (-0.5) * 1.4426950408889634
    column = lax.broadcasted_iota(jnp.int32, (1, span_text), 1)

    def fold(s, pick):
        m = s[:, :HD]
        for n in range(1, s.shape[1] // HD):
            m = pick(m, s[:, n * HD : (n + 1) * HD])
        return m

    def dot_t(a, b):
        return lax.dot_general(a, b, (((1,), (1,)), ((), ())), preferred_element_type=jnp.float32)

    def weigh(score, shift, value):
        weight = jnp.exp2((score - shift) * scale)
        product = jnp.dot(weight.astype(jnp.bfloat16), value, preferred_element_type=jnp.float32)
        return fold(weight, jnp.add), product

    def attend_group(c, i):
        q_part = q[c][i]
        text_at = span[i, 0]

        def text_of(buf):
            runs = [buf[text_at + n, :, c * HD : (c + 1) * HD] for n in range(span_text // trows)]
            return jnp.concatenate(runs, axis=0)

        off = [hidden[i, t] for t in range(G)]
        scores = [dot_t(q_part, k[c][t]) for t in range(G)]
        text_score = dot_t(q_part, text_of(tk))
        text_score = text_score + jnp.where(column < span[i, 1], 0.0, -LOW)
        top = fold(text_score, jnp.maximum)
        for t in range(G):
            top = jnp.maximum(top, fold(scores[t], jnp.maximum) - off[t])
        top = jnp.max(top, axis=1, keepdims=True)
        total, result = weigh(text_score, top, text_of(tv))
        for t in range(G):
            add, more = weigh(scores[t], top + off[t], v[c][t])
            total = total + add
            result = result + more
        top_a[c][i] = jnp.broadcast_to(top, (rows, HD))
        total_a[c][i] = total
        acc_a[c][i] = result

    def attend_around(c, r):
        i = member(r)
        q_part = q[c][i]
        total = total_a[c][i]
        result = acc_a[c][i]
        if around:
            off = [far_hidden[i, n] for n in range(around)]
            slots = [place[i, n] for n in range(around)]
            scores = [dot_t(q_part, far_k[c][slots[n]]) for n in range(around)]
            before = top_a[c][i]
            top = before
            for n in range(around):
                top = jnp.maximum(top, fold(scores[n], jnp.maximum) - off[n])
            top = jnp.max(top, axis=1, keepdims=True)
            fade = jnp.exp2((before - top) * scale)
            total = total * fade
            result = result * fade
            for n in range(around):
                add, more = weigh(scores[n], top + off[n], far_v[c][slots[n]])
                total = total + add
                result = result + more
        result = result / jnp.sum(total, axis=1, keepdims=True)
        sent[c][i] = result.astype(jnp.bfloat16)
        if G > 1:

            @pl.when(r > 0)
            def _():
                for d in range(n_head):
                    back_copy(c, r, d).start()

    def compute_group(c):
        def one(i, carry):
            attend_group(c, i)
            return carry

        lax.fori_loop(0, G, one, 0)

    own_rows = pl.ds(pl.multiple_of(head * out_rows, out_rows), out_rows)

    def compute_around(c):
        def one(n, carry):
            attend_around(c, G - 1 - n)
            return carry

        lax.fori_loop(0, G, one, 0)
        for d in range(1, n_head):
            back_copy(c, 0, d).start()
        attended[c][:, part(j * n_head + head, HD)] = sent[c][j, own_rows]

    def back_arrive(c, r):
        for d in range(n_head):
            if r + d > 0:
                back_copy(c, r, d).wait_recv()

    parts = 6 if wide % (6 * HD) == 0 else 1
    pw = wide // parts

    def project(c):
        def one(n, carry):
            cols = part(n, pw)
            add = jnp.dot(attended[c][...], w[c, :, cols], preferred_element_type=jnp.float32)
            acc[:, cols] = add if c == 0 else acc[:, cols] + add
            return carry

        lax.fori_loop(0, parts, one, 0, unroll=True)

    def out_copy(n):
        cols = part(n, pw)
        return pltpu.make_async_copy(mixed.at[:, cols], out_ref.at[:, cols], out_sem.at[n])

    def project_member(c, r, first, last):
        deep = pl.ds(pl.multiple_of(member(r) * n_head * HD, n_head * HD), n_head * HD)

        def one(n, carry):
            cols = part(n, pw)
            add = jnp.dot(attended[c][:, deep], w[c, deep, cols], preferred_element_type=jnp.float32)
            if not first:
                add = add + acc[:, cols]
            if last:
                mixed[:, cols] = add.astype(jnp.bfloat16)
                out_copy(n).start()
            else:
                acc[:, cols] = add
            return carry

        lax.fori_loop(0, parts, one, 0, unroll=True)

    def settle(c):
        for r in range(G):
            back_arrive(c, r)
        if c == 0:
            weight_each(weight_arrive)
        project(c)

    def weight_arrive(c, i, d):
        if d == 0:
            weight_copy(c, i, d).wait()
        else:
            weight_copy(c, i, d).wait_recv()

    for c in range(chunks):
        for r in peers:
            in_copy(c, r, 2).wait_recv()
        if c == 0:
            edge_each(chain_arrive)
        compute_group(c)
        if c + 1 < chunks:
            for s in range(2):
                take(c + 1, s)
            if c + 2 < chunks:
                for s in range(2):
                    forward(c + 2, 0, s)
        if 2 <= c:
            settle(c - 2)
        halo_arrive(c)
        compute_around(c)
    if chunks > 1:
        settle(chunks - 2)
    else:
        weight_each(weight_arrive)
    order = [3, 2, 0, 1] if G == PLANE else [0]
    for n, r in enumerate(order):
        back_arrive(chunks - 1, r)
        project_member(chunks - 1, r, chunks == 1 and n == 0, n == G - 1)

    for r in peers:
        list_copy(r).wait_send()
        for s in range(2):
            text_copy(r, s).wait_send()
        for c in range(chunks):
            for s in range(3):
                in_copy(c, r, s).wait_send()
            for d in range(n_head):
                back_copy(c, r, d).wait_send()
    for c in range(chunks):
        halo_done(c)

    def edge_done(by):
        @pl.when(group_exists(by))
        def _():
            for s in range(2):
                edge_copy(by, s).wait_send()

        if chained:

            @pl.when(group_exists(-by) & group_exists(by))
            def _():
                for s in range(2):
                    chain_copy(by, s).wait_send()

    edge_each(edge_done)
    for c in range(chunks):
        for d in range(1, n_head):
            back_copy(c, 0, d).wait_send()

    def weight_done(c, i, d):
        if d > 0:
            weight_copy(c, i, d).wait_send()

    weight_each(weight_done)
    for n in range(parts):
        out_copy(n).wait()


def body(n_seq, n_head, q, k, v, tk, tv, near, clip_lengths, text_lengths, w):
    rows, width = q.shape
    heads = width // HD
    G = group_of(n_seq, heads)
    chunks = heads // G
    wide = w.shape[1]
    out_rows = rows // n_head
    trows = tk.shape[0]
    span_text = -(-MOST * trows // HD) * HD
    hops = -(-REACH // G)
    text_hops = 1 if G < MOST - 1 <= 2 * G else -(-(MOST - 1) // G)
    others = max(G - 1, 1)
    window = max(G + 2 * (MOST - 1), G + MOST - 2 + span_text // trows)
    smem = pl.BlockSpec(memory_space=pltpu.SMEM)
    hbm = pl.BlockSpec(memory_space=pl.ANY)
    bf16, f32 = jnp.bfloat16, jnp.float32

    def pair(*shape):
        return [pltpu.SemaphoreType.DMA(shape), pltpu.SemaphoreType.DMA(shape)]

    return pl.pallas_call(
        functools.partial(kernel, n_seq, n_head),
        out_shape=jax.ShapeDtypeStruct((out_rows, wide), bf16),
        in_specs=[smem] * 3 + [hbm] * 6,
        out_specs=hbm,
        scratch_shapes=[
            [pltpu.VMEM((G, rows, HD), bf16) for _ in range(chunks)],
            [pltpu.VMEM((G, rows, HD), bf16) for _ in range(chunks)],
            [pltpu.VMEM((G, rows, HD), bf16) for _ in range(chunks)],
            [pltpu.VMEM((2 * REACH, rows, HD), bf16) for _ in range(chunks)],
            [pltpu.VMEM((2 * REACH, rows, HD), bf16) for _ in range(chunks)],
            pltpu.VMEM((window, trows, chunks * HD), bf16),
            pltpu.VMEM((window, trows, chunks * HD), bf16),
            pltpu.VMEM((chunks, n_head * G * HD, wide), bf16),
            [pltpu.VMEM((G, rows, HD), f32) for _ in range(chunks)],
            [pltpu.VMEM((G, rows, HD), f32) for _ in range(chunks)],
            [pltpu.VMEM((G, rows, HD), f32) for _ in range(chunks)],
            [pltpu.VMEM((G, rows, HD), bf16) for _ in range(chunks)],
            [pltpu.VMEM((out_rows, n_head * G * HD), bf16) for _ in range(chunks)],
            pltpu.VMEM((out_rows, wide), f32),
            pltpu.VMEM((out_rows, wide), bf16),
            pltpu.SMEM((G,) + near.shape, jnp.int32),
            pltpu.SMEM((G, near.shape[1]), jnp.int32),
            pltpu.SMEM((G, G), f32),
            pltpu.SMEM((G, near.shape[1]), f32),
            pltpu.SMEM((G, 2), jnp.int32),
            pair(others),
            pair(others, 2),
            pair(chunks, others, 3),
            pair(chunks, 2 * REACH, 2),
            pair(2, text_hops, 2),
            pair(2, 2),
            pair(chunks, G, n_head),
            pair(chunks * G, n_head - 1),
            pltpu.SemaphoreType.DMA((6,)),
            pltpu.SemaphoreType.DMA((3 * chunks + 2 + chunks * G,)),
        ],
        compiler_params=pltpu.CompilerParams(
            collective_id=0, has_side_effects=True, vmem_limit_bytes=58 << 20
        ),
    )(near, clip_lengths, text_lengths, q, k, v, tk, tv, w)


def solution(mesh):
    placed = (
        P("seq", "head"),
        P("seq", "head"),
        P("seq", "head"),
        P("seq", "head"),
        P("seq", "head"),
        P("seq", None),
        P(),
        P(),
        P("head", None),
    )
    return jax.shard_map(
        functools.partial(body, mesh.shape["seq"], mesh.shape["head"]),
        mesh=mesh,
        in_specs=placed,
        out_specs=P(("seq", "head"), None),
        check_vma=False,
    )
```

```python
import functools

import jax
import jax.numpy as jnp
from jax import lax
from jax.experimental import pallas as pl
from jax.experimental.pallas import tpu as pltpu
from jax.sharding import PartitionSpec as P

HD = 128
REACH = 3
MOST = 7
PLANE = 4
LOW = 1e30
MESH = pl.DeviceIdType.MESH


def group_of(n_seq, heads):
    return PLANE if n_seq % PLANE == 0 and heads % PLANE == 0 else 1


def kernel(
    n_seq,
    n_head,
    near_ref,
    clip_ref,
    text_ref,
    q_hbm,
    k_hbm,
    v_hbm,
    tk_hbm,
    tv_hbm,
    w_hbm,
    out_ref,
    q,
    k,
    v,
    far_k,
    far_v,
    tk,
    tv,
    w,
    top_a,
    total_a,
    acc_a,
    sent,
    attended,
    acc,
    mixed,
    lists,
    place,
    hidden,
    far_hidden,
    span,
    list_sem,
    text_sem,
    in_sem,
    halo_sem,
    edge_sem,
    chain_sem,
    back_sem,
    weight_sem,
    out_sem,
    local_sem,
):
    me = lax.axis_index("seq")
    head = lax.axis_index("head")
    rows, width = q_hbm.shape
    heads = width // HD
    G = group_of(n_seq, heads)
    groups = n_seq // G
    chunks = heads // G
    trows = tk_hbm.shape[0]
    tw = chunks * HD
    reach_text = MOST - 1
    span_text = -(-MOST * trows // HD) * HD
    entries = near_ref.shape[1]
    out_rows = rows // n_head
    wide = w_hbm.shape[1]
    j = lax.rem(me, G)
    mine = me // G
    base = me - j

    jx, jy = lax.rem(j, 2), j // 2

    def member(r):
        return 2 * lax.rem(jy + r // 2, 2) + lax.rem(jx + lax.rem(r, 2), 2) if G == PLANE else j

    peers = range(1, G)
    across_first = [3, 1, 2] if G == PLANE else []
    along_y_first = [2, 3, 1] if G == PLANE else []

    def part(i, size):
        return pl.ds(pl.multiple_of(i * size, HD), size)

    def push(src, dst, sem, at, to):
        return pltpu.make_async_remote_copy(
            src_ref=src,
            dst_ref=dst,
            send_sem=sem[0].at[at],
            recv_sem=sem[1].at[at],
            device_id=to,
            device_id_type=MESH,
        )

    def to_member(r):
        return {"seq": base + member(r)}

    def group_exists(by):
        return (mine + by >= 0) & (mine + by < groups)

    def list_copy(r):
        return push(near_ref, lists.at[j], list_sem, (r - 1,), to_member(r))

    def text_copy(r, s):
        src = (tk_hbm, tv_hbm)[s].at[:, part(member(r), tw)]
        dst = (tk, tv)[s].at[reach_text + j]
        return push(src, dst, text_sem, (r - 1, s), to_member(r))

    def in_copy(c, r, s):
        src = (k_hbm, v_hbm, q_hbm)[s].at[:, part(member(r) * chunks + c, HD)]
        dst = (k, v, q)[s][c].at[j]
        return push(src, dst, in_sem, (c, r - 1, s), to_member(r))

    around = 0 if groups == 1 else (2 if G == PLANE else entries - 1)
    hops = -(-REACH // G)
    chained = G < reach_text <= 2 * G
    text_hops = 1 if chained else -(-reach_text // G)

    def halo_copy(c, by, i, s):
        slot = REACH + i - by * G if by > 0 else REACH + i - by * G - G
        dst = (far_k, far_v)[s][c].at[slot]
        return push((k, v)[s][c].at[i], dst, halo_sem, (c, slot, s), {"seq": me + by * G})

    def halo_wanted(by, i):
        if by > 0:
            return by * G - i <= REACH
        return i - by * G - (G - 1) <= REACH

    def edge_copy(by, s):
        if by > 0:
            first = max(0, by * G - reach_text)
            count = G - first
        else:
            first = 0
            count = min(G, reach_text + by * G + G)
        src = (tk, tv)[s].at[pl.ds(reach_text + first, count)]
        dst = (tk, tv)[s].at[pl.ds(reach_text + first - by * G, count)]
        side = 0 if by > 0 else 1
        return push(src, dst, edge_sem, (side, abs(by) - 1, s), {"seq": me + by * G})

    def chain_copy(by, s):
        count = reach_text - G
        first = G if by > 0 else reach_text + G
        src = (tk, tv)[s].at[pl.ds(first, count)]
        dst = (tk, tv)[s].at[pl.ds(first - by * G, count)]
        return push(src, dst, chain_sem, (0 if by > 0 else 1, s), {"seq": me + by * G})

    def back_copy(c, r, d):
        to = lax.rem(head + d, n_head)
        src = sent[c].at[member(r), pl.ds(pl.multiple_of(to * out_rows, out_rows), out_rows)]
        dst = attended[c].at[:, part(j * n_head + head, HD)]
        return push(src, dst, back_sem, (c, r, d), {"seq": base + member(r), "head": to})

    def weight_copy(c, i, d):
        src = w_hbm.at[pl.ds((i * chunks + c) * HD, HD)]
        at = pl.ds(pl.multiple_of((i * n_head + head) * HD, HD), HD)
        if d == 0:
            return pltpu.make_async_copy(src, w.at[c, at], local_sem.at[3 * chunks + 2 + c * G + i])
        to = lax.rem(head + d, n_head)
        return push(src, w.at[c, at], weight_sem, (c * G + i, d - 1), {"head": to})

    def weight_each(act):
        for c in range(chunks):
            for i in range(G):
                for d in range(n_head):
                    act(c, i, d)

    own = []
    for c in range(chunks):
        for s, (hbm, buf) in enumerate(((k_hbm, k), (v_hbm, v), (q_hbm, q))):
            own.append(
                pltpu.make_async_copy(
                    hbm.at[:, part(j * chunks + c, HD)], buf[c].at[j], local_sem.at[3 * c + s]
                )
            )
    own_text = [
        pltpu.make_async_copy(
            hbm.at[:, part(j, tw)], buf.at[reach_text + j], local_sem.at[3 * chunks + s]
        )
        for s, (hbm, buf) in enumerate(((tk_hbm, tk), (tv_hbm, tv)))
    ]
    for copy in own:
        copy.start()
    tk[...] = jnp.zeros_like(tk)
    tv[...] = jnp.zeros_like(tv)
    for copy in own_text:
        copy.start()
    for e in range(entries):
        lists[j, 0, e] = near_ref[0, e]

    barrier = pltpu.get_barrier_semaphore()
    partners = jnp.int32(n_head * G - 1)
    for r in range(G):
        for d in range(n_head):
            if r + d > 0:
                to = {"seq": base + member(r), "head": lax.rem(head + d, n_head)}
                pl.semaphore_signal(barrier, inc=1, device_id=to, device_id_type=MESH)
    for step in range(1, max(hops, text_hops) + 1):
        for by in (step, -step):
            partners = partners + group_exists(by).astype(jnp.int32)

            @pl.when(group_exists(by))
            def _():
                pl.semaphore_signal(
                    barrier, inc=1, device_id={"seq": me + by * G}, device_id_type=MESH
                )

    for copy in own + own_text:
        copy.wait()
    pl.semaphore_wait(barrier, partners)

    def send_in(c, kinds):
        for s in kinds:
            for r in across_first:
                in_copy(c, r, s).start()

    def forward(c, r, s):
        i = member(r)
        for step in range(1, hops + 1):
            for by in (step, -step):

                @pl.when(group_exists(by) & halo_wanted(by, i))
                def _():
                    halo_copy(c, by, i, s).start()

    def take(c, s):
        for r in along_y_first:
            in_copy(c, r, s).wait_recv()
            forward(c, r, s)

    def halo_each(act):
        for step in range(1, hops + 1):
            for by in (step, -step):
                for i in range(G):
                    if halo_wanted(by, i):
                        act(by, i)

    def halo_arrive(c):
        def one(by, i):
            @pl.when(group_exists(-by))
            def _():
                for s in range(2):
                    halo_copy(c, by, i, s).wait_recv()

        halo_each(one)

    def halo_done(c):
        def one(by, i):
            @pl.when(group_exists(by))
            def _():
                for s in range(2):
                    halo_copy(c, by, i, s).wait_send()

        halo_each(one)

    def edge_each(act):
        for step in range(1, text_hops + 1):
            for by in (step, -step):
                act(by)

    for r in peers:
        list_copy(r).start()
    for s in range(2):
        for r in peers:
            text_copy(r, s).start()
    for c in range(chunks):
        send_in(c, (0, 1, 2))
    for s in range(2):
        forward(0, 0, s)

    def edge_start(by):
        @pl.when(group_exists(by))
        def _():
            for s in range(2):
                edge_copy(by, s).start()

    def edge_arrive(by):
        @pl.when(group_exists(-by))
        def _():
            for s in range(2):
                edge_copy(by, s).wait_recv()

        if chained:

            @pl.when(group_exists(-by) & group_exists(by))
            def _():
                for s in range(2):
                    chain_copy(by, s).start()

    def chain_arrive(by):
        if chained:

            @pl.when(group_exists(-2 * by))
            def _():
                for s in range(2):
                    chain_copy(by, s).wait_recv()

    for r in peers:
        for s in range(2):
            text_copy(r, s).wait_recv()
    edge_each(edge_start)
    take(0, 0)
    edge_each(edge_arrive)
    take(0, 1)
    weight_each(lambda c, i, d: weight_copy(c, i, d).start())
    if chunks > 1:
        for s in range(2):
            forward(1, 0, s)
    for r in peers:
        list_copy(r).wait_recv()

    spare = REACH - group_exists(-1).astype(jnp.int32)
    for i in range(G):
        tile = base + i
        for t in range(G):
            listed = lists[i, 0, 0] == base + t
            for e in range(1, entries):
                listed = listed | (lists[i, 0, e] == base + t)
            hidden[i, t] = (1.0 - listed.astype(jnp.float32)) * LOW
        slots = [jnp.int32(0) for _ in range(around)]
        count = jnp.int32(0)
        for e in range(entries):
            entry = lists[i, 0, e]
            rel = entry - base
            outside = (entry >= 0) & ((rel < 0) | (rel >= G))
            for before in range(e):
                outside = outside & (entry != lists[i, 0, before])
            outside = outside.astype(jnp.int32)
            slot = rel + REACH - G * (rel >= G).astype(jnp.int32)
            for n in range(around):
                slots[n] = slots[n] + outside * (count == n).astype(jnp.int32) * slot
            count = count + outside
        for n in range(around):
            used = (n < count).astype(jnp.int32)
            slot = used * slots[n] + (1 - used) * spare
            place[i, n] = jnp.maximum(jnp.minimum(slot, 2 * REACH - 1), 0)
            far_hidden[i, n] = (1.0 - used.astype(jnp.float32)) * LOW
        start = jnp.int32(0)
        first_tile = jnp.int32(0)
        count = jnp.int32(0)
        for c in range(clip_ref.shape[0]):
            length = clip_ref[c]
            inside = ((start <= tile) & (tile < start + length)).astype(jnp.int32)
            first_tile = first_tile + inside * start
            count = count + inside * text_ref[c]
            start = start + length
        span[i, 0] = jnp.maximum(jnp.minimum(first_tile - base, G - 1) + reach_text, 0)
        span[i, 1] = count

    scale = HD ** (-0.5) * 1.4426950408889634
    column = lax.broadcasted_iota(jnp.int32, (1, span_text), 1)

    def fold(s, pick):
        m = s[:, :HD]
        for n in range(1, s.shape[1] // HD):
            m = pick(m, s[:, n * HD : (n + 1) * HD])
        return m

    def dot_t(a, b):
        return lax.dot_general(a, b, (((1,), (1,)), ((), ())), preferred_element_type=jnp.float32)

    def weigh(score, shift, value):
        weight = jnp.exp2((score - shift) * scale)
        product = jnp.dot(weight.astype(jnp.bfloat16), value, preferred_element_type=jnp.float32)
        return fold(weight, jnp.add), product

    def attend_group(c, i):
        q_part = q[c][i]
        text_at = span[i, 0]

        def text_of(buf):
            runs = [buf[text_at + n, :, c * HD : (c + 1) * HD] for n in range(span_text // trows)]
            return jnp.concatenate(runs, axis=0)

        off = [hidden[i, t] for t in range(G)]
        scores = [dot_t(q_part, k[c][t]) for t in range(G)]
        text_score = dot_t(q_part, text_of(tk))
        text_score = text_score + jnp.where(column < span[i, 1], 0.0, -LOW)
        top = fold(text_score, jnp.maximum)
        for t in range(G):
            top = jnp.maximum(top, fold(scores[t], jnp.maximum) - off[t])
        top = jnp.max(top, axis=1, keepdims=True)
        total, result = weigh(text_score, top, text_of(tv))
        for t in range(G):
            add, more = weigh(scores[t], top + off[t], v[c][t])
            total = total + add
            result = result + more
        top_a[c][i] = jnp.broadcast_to(top, (rows, HD))
        total_a[c][i] = total
        acc_a[c][i] = result

    def attend_around(c, r):
        i = member(r)
        q_part = q[c][i]
        total = total_a[c][i]
        result = acc_a[c][i]
        if around:
            off = [far_hidden[i, n] for n in range(around)]
            slots = [place[i, n] for n in range(around)]
            scores = [dot_t(q_part, far_k[c][slots[n]]) for n in range(around)]
            before = top_a[c][i]
            top = before
            for n in range(around):
                top = jnp.maximum(top, fold(scores[n], jnp.maximum) - off[n])
            top = jnp.max(top, axis=1, keepdims=True)
            fade = jnp.exp2((before - top) * scale)
            total = total * fade
            result = result * fade
            for n in range(around):
                add, more = weigh(scores[n], top + off[n], far_v[c][slots[n]])
                total = total + add
                result = result + more
        result = result / jnp.sum(total, axis=1, keepdims=True)
        sent[c][i] = result.astype(jnp.bfloat16)
        if G > 1:

            @pl.when(r > 0)
            def _():
                for d in range(n_head):
                    back_copy(c, r, d).start()

    def compute_group(c):
        def one(i, carry):
            attend_group(c, i)
            return carry

        lax.fori_loop(0, G, one, 0, unroll=min(2, G))

    own_rows = pl.ds(pl.multiple_of(head * out_rows, out_rows), out_rows)

    def compute_around(c):
        def one(n, carry):
            attend_around(c, G - 1 - n)
            return carry

        lax.fori_loop(0, G, one, 0, unroll=min(2, G))
        for d in range(1, n_head):
            back_copy(c, 0, d).start()
        attended[c][:, part(j * n_head + head, HD)] = sent[c][j, own_rows]

    def back_arrive(c, r):
        for d in range(n_head):
            if r + d > 0:
                back_copy(c, r, d).wait_recv()

    parts = 6 if wide % (6 * HD) == 0 else 1
    pw = wide // parts

    def project(c):
        def one(n, carry):
            cols = part(n, pw)
            add = jnp.dot(attended[c][...], w[c, :, cols], preferred_element_type=jnp.float32)
            acc[:, cols] = add if c == 0 else acc[:, cols] + add
            return carry

        lax.fori_loop(0, parts, one, 0, unroll=True)

    def out_copy(n):
        cols = part(n, pw)
        return pltpu.make_async_copy(mixed.at[:, cols], out_ref.at[:, cols], out_sem.at[n])

    def project_members(c, which, first, last):
        runs = [
            pl.ds(pl.multiple_of(member(r) * n_head * HD, n_head * HD), n_head * HD) for r in which
        ]

        def one(n, carry):
            cols = part(n, pw)
            a = jnp.concatenate([attended[c][:, run] for run in runs], axis=1)
            b = jnp.concatenate([w[c, run, cols] for run in runs], axis=0)
            add = jnp.dot(a, b, preferred_element_type=jnp.float32)
            if not first:
                add = add + acc[:, cols]
            if last:
                mixed[:, cols] = add.astype(jnp.bfloat16)
                out_copy(n).start()
            else:
                acc[:, cols] = add
            return carry

        lax.fori_loop(0, parts, one, 0, unroll=True)

    def settle(c):
        for r in range(G):
            back_arrive(c, r)
        if c == 0:
            weight_each(weight_arrive)
        project(c)

    def weight_arrive(c, i, d):
        if d == 0:
            weight_copy(c, i, d).wait()
        else:
            weight_copy(c, i, d).wait_recv()

    for c in range(chunks):
        for r in peers:
            in_copy(c, r, 2).wait_recv()
        if c == 0:
            edge_each(chain_arrive)
        compute_group(c)
        if c + 1 < chunks:
            for s in range(2):
                take(c + 1, s)
            if c + 2 < chunks:
                for s in range(2):
                    forward(c + 2, 0, s)
        if 2 <= c:
            settle(c - 2)
        halo_arrive(c)
        compute_around(c)
    if chunks > 1:
        settle(chunks - 2)
    else:
        weight_each(weight_arrive)
    turns = [[3, 2, 0], [1]] if G == PLANE else [[0]]
    for n, which in enumerate(turns):
        for r in which:
            back_arrive(chunks - 1, r)
        project_members(chunks - 1, which, chunks == 1 and n == 0, n == len(turns) - 1)

    for r in peers:
        list_copy(r).wait_send()
        for s in range(2):
            text_copy(r, s).wait_send()
        for c in range(chunks):
            for s in range(3):
                in_copy(c, r, s).wait_send()
            for d in range(n_head):
                back_copy(c, r, d).wait_send()
    for c in range(chunks):
        halo_done(c)

    def edge_done(by):
        @pl.when(group_exists(by))
        def _():
            for s in range(2):
                edge_copy(by, s).wait_send()

        if chained:

            @pl.when(group_exists(-by) & group_exists(by))
            def _():
                for s in range(2):
                    chain_copy(by, s).wait_send()

    edge_each(edge_done)
    for c in range(chunks):
        for d in range(1, n_head):
            back_copy(c, 0, d).wait_send()

    def weight_done(c, i, d):
        if d > 0:
            weight_copy(c, i, d).wait_send()

    weight_each(weight_done)
    for n in range(parts):
        out_copy(n).wait()


def body(n_seq, n_head, q, k, v, tk, tv, near, clip_lengths, text_lengths, w):
    rows, width = q.shape
    heads = width // HD
    G = group_of(n_seq, heads)
    chunks = heads // G
    wide = w.shape[1]
    out_rows = rows // n_head
    trows = tk.shape[0]
    span_text = -(-MOST * trows // HD) * HD
    hops = -(-REACH // G)
    text_hops = 1 if G < MOST - 1 <= 2 * G else -(-(MOST - 1) // G)
    others = max(G - 1, 1)
    window = max(G + 2 * (MOST - 1), G + MOST - 2 + span_text // trows)
    smem = pl.BlockSpec(memory_space=pltpu.SMEM)
    hbm = pl.BlockSpec(memory_space=pl.ANY)
    bf16, f32 = jnp.bfloat16, jnp.float32

    def pair(*shape):
        return [pltpu.SemaphoreType.DMA(shape), pltpu.SemaphoreType.DMA(shape)]

    return pl.pallas_call(
        functools.partial(kernel, n_seq, n_head),
        out_shape=jax.ShapeDtypeStruct((out_rows, wide), bf16),
        in_specs=[smem] * 3 + [hbm] * 6,
        out_specs=hbm,
        scratch_shapes=[
            [pltpu.VMEM((G, rows, HD), bf16) for _ in range(chunks)],
            [pltpu.VMEM((G, rows, HD), bf16) for _ in range(chunks)],
            [pltpu.VMEM((G, rows, HD), bf16) for _ in range(chunks)],
            [pltpu.VMEM((2 * REACH, rows, HD), bf16) for _ in range(chunks)],
            [pltpu.VMEM((2 * REACH, rows, HD), bf16) for _ in range(chunks)],
            pltpu.VMEM((window, trows, chunks * HD), bf16),
            pltpu.VMEM((window, trows, chunks * HD), bf16),
            pltpu.VMEM((chunks, n_head * G * HD, wide), bf16),
            [pltpu.VMEM((G, rows, HD), f32) for _ in range(chunks)],
            [pltpu.VMEM((G, rows, HD), f32) for _ in range(chunks)],
            [pltpu.VMEM((G, rows, HD), f32) for _ in range(chunks)],
            [pltpu.VMEM((G, rows, HD), bf16) for _ in range(chunks)],
            [pltpu.VMEM((out_rows, n_head * G * HD), bf16) for _ in range(chunks)],
            pltpu.VMEM((out_rows, wide), f32),
            pltpu.VMEM((out_rows, wide), bf16),
            pltpu.SMEM((G,) + near.shape, jnp.int32),
            pltpu.SMEM((G, near.shape[1]), jnp.int32),
            pltpu.SMEM((G, G), f32),
            pltpu.SMEM((G, near.shape[1]), f32),
            pltpu.SMEM((G, 2), jnp.int32),
            pair(others),
            pair(others, 2),
            pair(chunks, others, 3),
            pair(chunks, 2 * REACH, 2),
            pair(2, text_hops, 2),
            pair(2, 2),
            pair(chunks, G, n_head),
            pair(chunks * G, n_head - 1),
            pltpu.SemaphoreType.DMA((6,)),
            pltpu.SemaphoreType.DMA((3 * chunks + 2 + chunks * G,)),
        ],
        compiler_params=pltpu.CompilerParams(
            collective_id=0, has_side_effects=True, vmem_limit_bytes=58 << 20
        ),
    )(near, clip_lengths, text_lengths, q, k, v, tk, tv, w)


def solution(mesh):
    placed = (
        P("seq", "head"),
        P("seq", "head"),
        P("seq", "head"),
        P("seq", "head"),
        P("seq", "head"),
        P("seq", None),
        P(),
        P(),
        P("head", None),
    )
    return jax.shard_map(
        functools.partial(body, mesh.shape["seq"], mesh.shape["head"]),
        mesh=mesh,
        in_specs=placed,
        out_specs=P(("seq", "head"), None),
        check_vma=False,
    )
```

```python
import functools

import jax
import jax.numpy as jnp
from jax import lax
from jax.experimental import pallas as pl
from jax.experimental.pallas import tpu as pltpu
from jax.sharding import PartitionSpec as P

HD = 128
REACH = 3
MOST = 7
PLANE = 4
LOW = 1e30
MESH = pl.DeviceIdType.MESH


def group_of(n_seq, heads):
    return PLANE if n_seq % PLANE == 0 and heads % PLANE == 0 else 1


def kernel(
    n_seq,
    n_head,
    near_ref,
    clip_ref,
    text_ref,
    q_hbm,
    k_hbm,
    v_hbm,
    tk_hbm,
    tv_hbm,
    w_hbm,
    out_ref,
    q,
    k,
    v,
    far_k,
    far_v,
    tk,
    tv,
    w,
    top_a,
    total_a,
    acc_a,
    sent,
    attended,
    acc,
    mixed,
    lists,
    place,
    hidden,
    far_hidden,
    span,
    list_sem,
    text_sem,
    in_sem,
    halo_sem,
    edge_sem,
    chain_sem,
    back_sem,
    weight_sem,
    out_sem,
    local_sem,
):
    me = lax.axis_index("seq")
    head = lax.axis_index("head")
    rows, width = q_hbm.shape
    heads = width // HD
    G = group_of(n_seq, heads)
    groups = n_seq // G
    chunks = heads // G
    trows = tk_hbm.shape[0]
    tw = chunks * HD
    reach_text = MOST - 1
    span_text = -(-MOST * trows // HD) * HD
    entries = near_ref.shape[1]
    out_rows = rows // n_head
    wide = w_hbm.shape[1]
    j = lax.rem(me, G)
    mine = me // G
    base = me - j

    jx, jy = lax.rem(j, 2), j // 2

    def member(r):
        return 2 * lax.rem(jy + r // 2, 2) + lax.rem(jx + lax.rem(r, 2), 2) if G == PLANE else j

    peers = range(1, G)
    across_first = [3, 1, 2] if G == PLANE else []
    along_y_first = [2, 3, 1] if G == PLANE else []

    def part(i, size):
        return pl.ds(pl.multiple_of(i * size, HD), size)

    def push(src, dst, sem, at, to):
        return pltpu.make_async_remote_copy(
            src_ref=src,
            dst_ref=dst,
            send_sem=sem[0].at[at],
            recv_sem=sem[1].at[at],
            device_id=to,
            device_id_type=MESH,
        )

    def to_member(r):
        return {"seq": base + member(r)}

    def group_exists(by):
        return (mine + by >= 0) & (mine + by < groups)

    def list_copy(r):
        return push(near_ref, lists.at[j], list_sem, (r - 1,), to_member(r))

    def text_copy(r, s):
        src = (tk_hbm, tv_hbm)[s].at[:, part(member(r), tw)]
        dst = (tk, tv)[s].at[reach_text + j]
        return push(src, dst, text_sem, (r - 1, s), to_member(r))

    def in_copy(c, r, s):
        src = (k_hbm, v_hbm, q_hbm)[s].at[:, part(member(r) * chunks + c, HD)]
        dst = (k, v, q)[s][c].at[j]
        return push(src, dst, in_sem, (c, r - 1, s), to_member(r))

    around = 0 if groups == 1 else (2 if G == PLANE else entries - 1)
    hops = -(-REACH // G)
    chained = G < reach_text <= 2 * G
    text_hops = 1 if chained else -(-reach_text // G)

    def halo_copy(c, by, i, s):
        slot = REACH + i - by * G if by > 0 else REACH + i - by * G - G
        dst = (far_k, far_v)[s][c].at[slot]
        return push((k, v)[s][c].at[i], dst, halo_sem, (c, slot, s), {"seq": me + by * G})

    def halo_wanted(by, i):
        if by > 0:
            return by * G - i <= REACH
        return i - by * G - (G - 1) <= REACH

    def edge_copy(by, s):
        if by > 0:
            first = max(0, by * G - reach_text)
            count = G - first
        else:
            first = 0
            count = min(G, reach_text + by * G + G)
        src = (tk, tv)[s].at[pl.ds(reach_text + first, count)]
        dst = (tk, tv)[s].at[pl.ds(reach_text + first - by * G, count)]
        side = 0 if by > 0 else 1
        return push(src, dst, edge_sem, (side, abs(by) - 1, s), {"seq": me + by * G})

    def chain_copy(by, s):
        count = reach_text - G
        first = G if by > 0 else reach_text + G
        src = (tk, tv)[s].at[pl.ds(first, count)]
        dst = (tk, tv)[s].at[pl.ds(first - by * G, count)]
        return push(src, dst, chain_sem, (0 if by > 0 else 1, s), {"seq": me + by * G})

    def back_copy(c, r, d):
        to = lax.rem(head + d, n_head)
        src = sent[c].at[member(r), pl.ds(pl.multiple_of(to * out_rows, out_rows), out_rows)]
        dst = attended[c].at[:, part(j * n_head + head, HD)]
        return push(src, dst, back_sem, (c, r, d), {"seq": base + member(r), "head": to})

    def weight_copy(c, i, d):
        src = w_hbm.at[pl.ds((i * chunks + c) * HD, HD)]
        at = pl.ds(pl.multiple_of((i * n_head + head) * HD, HD), HD)
        if d == 0:
            return pltpu.make_async_copy(src, w.at[c, at], local_sem.at[3 * chunks + 2 + c * G + i])
        to = lax.rem(head + d, n_head)
        return push(src, w.at[c, at], weight_sem, (c * G + i, d - 1), {"head": to})

    def weight_each(act):
        for c in range(chunks):
            for i in range(G):
                for d in range(n_head):
                    act(c, i, d)

    own = []
    for c in range(chunks):
        for s, (hbm, buf) in enumerate(((k_hbm, k), (v_hbm, v), (q_hbm, q))):
            own.append(
                pltpu.make_async_copy(
                    hbm.at[:, part(j * chunks + c, HD)], buf[c].at[j], local_sem.at[3 * c + s]
                )
            )
    own_text = [
        pltpu.make_async_copy(
            hbm.at[:, part(j, tw)], buf.at[reach_text + j], local_sem.at[3 * chunks + s]
        )
        for s, (hbm, buf) in enumerate(((tk_hbm, tk), (tv_hbm, tv)))
    ]
    for copy in own:
        copy.start()
    tk[...] = jnp.zeros_like(tk)
    tv[...] = jnp.zeros_like(tv)
    for copy in own_text:
        copy.start()
    for e in range(entries):
        lists[j, 0, e] = near_ref[0, e]

    barrier = pltpu.get_barrier_semaphore()
    partners = jnp.int32(n_head * G - 1)
    for r in range(G):
        for d in range(n_head):
            if r + d > 0:
                to = {"seq": base + member(r), "head": lax.rem(head + d, n_head)}
                pl.semaphore_signal(barrier, inc=1, device_id=to, device_id_type=MESH)
    for step in range(1, max(hops, text_hops) + 1):
        for by in (step, -step):
            partners = partners + group_exists(by).astype(jnp.int32)

            @pl.when(group_exists(by))
            def _():
                pl.semaphore_signal(
                    barrier, inc=1, device_id={"seq": me + by * G}, device_id_type=MESH
                )

    for copy in own + own_text:
        copy.wait()
    pl.semaphore_wait(barrier, partners)

    def send_in(c, kinds):
        for s in kinds:
            for r in across_first:
                in_copy(c, r, s).start()

    def forward(c, r, s):
        i = member(r)
        for step in range(1, hops + 1):
            for by in (step, -step):

                @pl.when(group_exists(by) & halo_wanted(by, i))
                def _():
                    halo_copy(c, by, i, s).start()

    def take(c, s):
        for r in along_y_first:
            in_copy(c, r, s).wait_recv()
            forward(c, r, s)

    def halo_each(act):
        for step in range(1, hops + 1):
            for by in (step, -step):
                for i in range(G):
                    if halo_wanted(by, i):
                        act(by, i)

    def halo_arrive(c):
        def one(by, i):
            @pl.when(group_exists(-by))
            def _():
                for s in range(2):
                    halo_copy(c, by, i, s).wait_recv()

        halo_each(one)

    def halo_done(c):
        def one(by, i):
            @pl.when(group_exists(by))
            def _():
                for s in range(2):
                    halo_copy(c, by, i, s).wait_send()

        halo_each(one)

    def edge_each(act):
        for step in range(1, text_hops + 1):
            for by in (step, -step):
                act(by)

    for r in peers:
        list_copy(r).start()
    for s in range(2):
        for r in peers:
            text_copy(r, s).start()
    for c in range(chunks):
        send_in(c, (0, 1, 2))
    for s in range(2):
        forward(0, 0, s)

    def edge_start(by):
        @pl.when(group_exists(by))
        def _():
            for s in range(2):
                edge_copy(by, s).start()

    def edge_arrive(by):
        @pl.when(group_exists(-by))
        def _():
            for s in range(2):
                edge_copy(by, s).wait_recv()

        if chained:

            @pl.when(group_exists(-by) & group_exists(by))
            def _():
                for s in range(2):
                    chain_copy(by, s).start()

    def chain_arrive(by):
        if chained:

            @pl.when(group_exists(-2 * by))
            def _():
                for s in range(2):
                    chain_copy(by, s).wait_recv()

    for r in peers:
        for s in range(2):
            text_copy(r, s).wait_recv()
    edge_each(edge_start)
    take(0, 0)
    edge_each(edge_arrive)
    take(0, 1)
    weight_each(lambda c, i, d: weight_copy(c, i, d).start())
    if chunks > 1:
        for s in range(2):
            forward(1, 0, s)
    for r in peers:
        list_copy(r).wait_recv()

    spare = REACH - group_exists(-1).astype(jnp.int32)
    for i in range(G):
        tile = base + i
        for t in range(G):
            listed = lists[i, 0, 0] == base + t
            for e in range(1, entries):
                listed = listed | (lists[i, 0, e] == base + t)
            hidden[i, t] = (1.0 - listed.astype(jnp.float32)) * LOW
        slots = [jnp.int32(0) for _ in range(around)]
        count = jnp.int32(0)
        for e in range(entries):
            entry = lists[i, 0, e]
            rel = entry - base
            outside = (entry >= 0) & ((rel < 0) | (rel >= G))
            for before in range(e):
                outside = outside & (entry != lists[i, 0, before])
            outside = outside.astype(jnp.int32)
            slot = rel + REACH - G * (rel >= G).astype(jnp.int32)
            for n in range(around):
                slots[n] = slots[n] + outside * (count == n).astype(jnp.int32) * slot
            count = count + outside
        for n in range(around):
            used = (n < count).astype(jnp.int32)
            slot = used * slots[n] + (1 - used) * spare
            place[i, n] = jnp.maximum(jnp.minimum(slot, 2 * REACH - 1), 0)
            far_hidden[i, n] = (1.0 - used.astype(jnp.float32)) * LOW
        start = jnp.int32(0)
        first_tile = jnp.int32(0)
        count = jnp.int32(0)
        for c in range(clip_ref.shape[0]):
            length = clip_ref[c]
            inside = ((start <= tile) & (tile < start + length)).astype(jnp.int32)
            first_tile = first_tile + inside * start
            count = count + inside * text_ref[c]
            start = start + length
        span[i, 0] = jnp.maximum(jnp.minimum(first_tile - base, G - 1) + reach_text, 0)
        span[i, 1] = count

    scale = HD ** (-0.5) * 1.4426950408889634
    column = lax.broadcasted_iota(jnp.int32, (1, span_text), 1)

    def fold(s, pick):
        m = s[:, :HD]
        for n in range(1, s.shape[1] // HD):
            m = pick(m, s[:, n * HD : (n + 1) * HD])
        return m

    def dot_t(a, b):
        return lax.dot_general(a, b, (((1,), (1,)), ((), ())), preferred_element_type=jnp.float32)

    def weigh(score, shift, value):
        weight = jnp.exp2((score - shift) * scale)
        product = jnp.dot(weight.astype(jnp.bfloat16), value, preferred_element_type=jnp.float32)
        return fold(weight, jnp.add), product

    def attend_group(c, i):
        q_part = q[c][i]
        text_at = span[i, 0]

        def text_of(buf):
            runs = [buf[text_at + n, :, c * HD : (c + 1) * HD] for n in range(span_text // trows)]
            return jnp.concatenate(runs, axis=0)

        off = [hidden[i, t] for t in range(G)]
        scores = [dot_t(q_part, k[c][t]) for t in range(G)]
        text_score = dot_t(q_part, text_of(tk))
        text_score = text_score + jnp.where(column < span[i, 1], 0.0, -LOW)
        top = fold(text_score, jnp.maximum)
        for t in range(G):
            top = jnp.maximum(top, fold(scores[t], jnp.maximum) - off[t])
        top = jnp.max(top, axis=1, keepdims=True)
        total, result = weigh(text_score, top, text_of(tv))
        for t in range(G):
            add, more = weigh(scores[t], top + off[t], v[c][t])
            total = total + add
            result = result + more
        top_a[c][i] = jnp.broadcast_to(top, (rows, HD))
        total_a[c][i] = total
        acc_a[c][i] = result

    def attend_around(c, r):
        i = member(r)
        q_part = q[c][i]
        total = total_a[c][i]
        result = acc_a[c][i]
        if around:
            off = [far_hidden[i, n] for n in range(around)]
            slots = [place[i, n] for n in range(around)]
            scores = [dot_t(q_part, far_k[c][slots[n]]) for n in range(around)]
            before = top_a[c][i]
            top = before
            for n in range(around):
                top = jnp.maximum(top, fold(scores[n], jnp.maximum) - off[n])
            top = jnp.max(top, axis=1, keepdims=True)
            fade = jnp.exp2((before - top) * scale)
            total = total * fade
            result = result * fade
            for n in range(around):
                add, more = weigh(scores[n], top + off[n], far_v[c][slots[n]])
                total = total + add
                result = result + more
        result = result / jnp.sum(total, axis=1, keepdims=True)
        sent[c][i] = result.astype(jnp.bfloat16)
        if G > 1:

            @pl.when(r > 0)
            def _():
                for d in range(n_head):
                    back_copy(c, r, d).start()

    def compute_group(c):
        def one(i, carry):
            attend_group(c, i)
            return carry

        lax.fori_loop(0, G, one, 0, unroll=min(2, G))

    own_rows = pl.ds(pl.multiple_of(head * out_rows, out_rows), out_rows)

    def compute_around(c):
        def one(n, carry):
            attend_around(c, G - 1 - n)
            return carry

        lax.fori_loop(0, G, one, 0, unroll=min(2, G))
        for d in range(1, n_head):
            back_copy(c, 0, d).start()
        attended[c][:, part(j * n_head + head, HD)] = sent[c][j, own_rows]

    def back_arrive(c, r):
        for d in range(n_head):
            if r + d > 0:
                back_copy(c, r, d).wait_recv()

    parts = 3 if wide % (3 * HD) == 0 else 1
    pw = wide // parts

    def project(c):
        def one(n, carry):
            cols = part(n, pw)
            add = jnp.dot(attended[c][...], w[c, :, cols], preferred_element_type=jnp.float32)
            acc[:, cols] = add if c == 0 else acc[:, cols] + add
            return carry

        lax.fori_loop(0, parts, one, 0, unroll=True)

    def out_copy(n):
        cols = part(n, pw)
        return pltpu.make_async_copy(mixed.at[:, cols], out_ref.at[:, cols], out_sem.at[n])

    def project_members(c, which, first, last):
        runs = [
            pl.ds(pl.multiple_of(member(r) * n_head * HD, n_head * HD), n_head * HD) for r in which
        ]

        def one(n, carry):
            cols = part(n, pw)
            a = jnp.concatenate([attended[c][:, run] for run in runs], axis=1)
            b = jnp.concatenate([w[c, run, cols] for run in runs], axis=0)
            add = jnp.dot(a, b, preferred_element_type=jnp.float32)
            if not first:
                add = add + acc[:, cols]
            if last:
                mixed[:, cols] = add.astype(jnp.bfloat16)
                out_copy(n).start()
            else:
                acc[:, cols] = add
            return carry

        lax.fori_loop(0, parts, one, 0, unroll=True)

    def settle(c):
        for r in range(G):
            back_arrive(c, r)
        if c == 0:
            weight_each(weight_arrive)
        project(c)

    def weight_arrive(c, i, d):
        if d == 0:
            weight_copy(c, i, d).wait()
        else:
            weight_copy(c, i, d).wait_recv()

    for c in range(chunks):
        for r in peers:
            in_copy(c, r, 2).wait_recv()
        if c == 0:
            edge_each(chain_arrive)
        compute_group(c)
        if c + 1 < chunks:
            for s in range(2):
                take(c + 1, s)
            if c + 2 < chunks:
                for s in range(2):
                    forward(c + 2, 0, s)
        if 2 <= c:
            settle(c - 2)
        halo_arrive(c)
        compute_around(c)
    if chunks > 1:
        settle(chunks - 2)
    else:
        weight_each(weight_arrive)
    turns = [[3, 2, 0], [1]] if G == PLANE else [[0]]
    for n, which in enumerate(turns):
        for r in which:
            back_arrive(chunks - 1, r)
        project_members(chunks - 1, which, chunks == 1 and n == 0, n == len(turns) - 1)

    for r in peers:
        list_copy(r).wait_send()
        for s in range(2):
            text_copy(r, s).wait_send()
        for c in range(chunks):
            for s in range(3):
                in_copy(c, r, s).wait_send()
            for d in range(n_head):
                back_copy(c, r, d).wait_send()
    for c in range(chunks):
        halo_done(c)

    def edge_done(by):
        @pl.when(group_exists(by))
        def _():
            for s in range(2):
                edge_copy(by, s).wait_send()

        if chained:

            @pl.when(group_exists(-by) & group_exists(by))
            def _():
                for s in range(2):
                    chain_copy(by, s).wait_send()

    edge_each(edge_done)
    for c in range(chunks):
        for d in range(1, n_head):
            back_copy(c, 0, d).wait_send()

    def weight_done(c, i, d):
        if d > 0:
            weight_copy(c, i, d).wait_send()

    weight_each(weight_done)
    for n in range(parts):
        out_copy(n).wait()


def body(n_seq, n_head, q, k, v, tk, tv, near, clip_lengths, text_lengths, w):
    rows, width = q.shape
    heads = width // HD
    G = group_of(n_seq, heads)
    chunks = heads // G
    wide = w.shape[1]
    out_rows = rows // n_head
    trows = tk.shape[0]
    span_text = -(-MOST * trows // HD) * HD
    hops = -(-REACH // G)
    text_hops = 1 if G < MOST - 1 <= 2 * G else -(-(MOST - 1) // G)
    others = max(G - 1, 1)
    window = max(G + 2 * (MOST - 1), G + MOST - 2 + span_text // trows)
    smem = pl.BlockSpec(memory_space=pltpu.SMEM)
    hbm = pl.BlockSpec(memory_space=pl.ANY)
    bf16, f32 = jnp.bfloat16, jnp.float32

    def pair(*shape):
        return [pltpu.SemaphoreType.DMA(shape), pltpu.SemaphoreType.DMA(shape)]

    return pl.pallas_call(
        functools.partial(kernel, n_seq, n_head),
        out_shape=jax.ShapeDtypeStruct((out_rows, wide), bf16),
        in_specs=[smem] * 3 + [hbm] * 6,
        out_specs=hbm,
        scratch_shapes=[
            [pltpu.VMEM((G, rows, HD), bf16) for _ in range(chunks)],
            [pltpu.VMEM((G, rows, HD), bf16) for _ in range(chunks)],
            [pltpu.VMEM((G, rows, HD), bf16) for _ in range(chunks)],
            [pltpu.VMEM((2 * REACH, rows, HD), bf16) for _ in range(chunks)],
            [pltpu.VMEM((2 * REACH, rows, HD), bf16) for _ in range(chunks)],
            pltpu.VMEM((window, trows, chunks * HD), bf16),
            pltpu.VMEM((window, trows, chunks * HD), bf16),
            pltpu.VMEM((chunks, n_head * G * HD, wide), bf16),
            [pltpu.VMEM((G, rows, HD), f32) for _ in range(chunks)],
            [pltpu.VMEM((G, rows, HD), f32) for _ in range(chunks)],
            [pltpu.VMEM((G, rows, HD), f32) for _ in range(chunks)],
            [pltpu.VMEM((G, rows, HD), bf16) for _ in range(chunks)],
            [pltpu.VMEM((out_rows, n_head * G * HD), bf16) for _ in range(chunks)],
            pltpu.VMEM((out_rows, wide), f32),
            pltpu.VMEM((out_rows, wide), bf16),
            pltpu.SMEM((G,) + near.shape, jnp.int32),
            pltpu.SMEM((G, near.shape[1]), jnp.int32),
            pltpu.SMEM((G, G), f32),
            pltpu.SMEM((G, near.shape[1]), f32),
            pltpu.SMEM((G, 2), jnp.int32),
            pair(others),
            pair(others, 2),
            pair(chunks, others, 3),
            pair(chunks, 2 * REACH, 2),
            pair(2, text_hops, 2),
            pair(2, 2),
            pair(chunks, G, n_head),
            pair(chunks * G, n_head - 1),
            pltpu.SemaphoreType.DMA((6,)),
            pltpu.SemaphoreType.DMA((3 * chunks + 2 + chunks * G,)),
        ],
        compiler_params=pltpu.CompilerParams(
            collective_id=0, has_side_effects=True, vmem_limit_bytes=58 << 20
        ),
    )(near, clip_lengths, text_lengths, q, k, v, tk, tv, w)


def solution(mesh):
    placed = (
        P("seq", "head"),
        P("seq", "head"),
        P("seq", "head"),
        P("seq", "head"),
        P("seq", "head"),
        P("seq", None),
        P(),
        P(),
        P("head", None),
    )
    return jax.shard_map(
        functools.partial(body, mesh.shape["seq"], mesh.shape["head"]),
        mesh=mesh,
        in_specs=placed,
        out_specs=P(("seq", "head"), None),
        check_vma=False,
    )
```
